512 devices in a mesh: stn: 16 (over z, core), chan: 32 (over y, x).
Axes of the slice: x: 4, y: 8, z: 8, core: 2. Of those that a mesh axis runs over, the one named last changes fastest.
Arguments:
- voltages: bfloat16 [256, 2048, 512], P('stn', 'chan'), may hold values from -6 to 6
- block_facet: int32 [32, 16, 2048, 1], P('chan', 'stn'), may hold values from 0 to 15; in each aligned block of 2048 rows (0 to 2047, 2048 to 4095, ..., all dimensions but the last counted through in order) at most 192 rows name the same one
- block_tile: int32 [32, 16, 2048], P('chan', 'stn'), may hold values from 0 to 15
- vis_offset: int32 [32, 16, 2048, 128], P('chan', 'stn'), may hold values from 0 to 624
- kernel_taps: bfloat16 [2, 8], replicated, may hold values from 0.19921875 to 1
Outputs:
- image: float32 [2, 2048, 128], P(None, ('stn', 'chan'))
The draws below stay inside these ranges and needn't reach their ends.
Inputs may be any that keep to these rules, and one draw needn't show every extreme that they name: `block_facet`: among the blocks of one device (one index of the first two dimensions) at most 192 name one facet; in every draw some facet is named by exactly 192 of some device's blocks.
All inputs are finite; a program needn't handle non-finite values.
Results may differ from the reference program's by a relative error of at most 0.0041.
Values may be sent and summed in bfloat16 or wider, within the bound.
A program may use at most 64 MiB of HBM per device.

```python
import math
import jax
import jax.numpy as jnp
import numpy as np
from jax import lax

STATIONS = 256
SAMPLES = 256
VB = 128
TILE = 32
KT = 8
TS = 4
FACETS = 16
CGROUPS = 32
CHANNELS = 2048
BLK_DEV = 2048
CAP = 192
TT = 16
FG = 128
OFFS = 25


def with_ends(entries, rng, least, high):
    place = [jax.random.randint(jax.random.fold_in(rng, axis), (), 0, length) for axis, length in enumerate(entries.shape)]
    main_axis = entries.shape.index(max(entries.shape))
    neighbour = place[:main_axis] + [(place[main_axis] + 1) % entries.shape[main_axis]] + place[main_axis + 1:]
    return entries.at[tuple(place)].set(least).at[tuple(neighbour)].set(high)


def shard_levels(own_key, extent, shards, smallest, top_value):
    loudness = 1.0
    for dim, parts in shards:
        heights = jax.random.uniform(jax.random.fold_in(jax.random.fold_in(own_key, 6), dim), (parts,), jnp.float32, smallest / len(shards), top_value / len(shards))
        loudness = loudness * jnp.repeat(jnp.exp(heights), extent[dim] // parts).reshape((-1,) + (1,) * (len(extent) - 1 - dim))
    return loudness


def deal_out(key, own, number, rows, count, top, most, skew):
    ranking = jax.random.permutation(key, count)
    packed, usual = shares(count, rows * top, most, skew, True), shares(count, rows * top, most, skew, False)
    places = jnp.arange(count)

    def named(tallies, rotation):
        used = int((tallies > 0).sum())
        fixed = max(1, used // 4)
        moved = fixed + (places - fixed + rotation * (used - fixed)) % max(1, count - fixed)
        return jnp.zeros((count,), jnp.int32).at[ranking[jnp.where(places < fixed, places, moved)]].set(jnp.asarray(tallies, jnp.int32))

    tallies = jnp.where(number % 4 == 0, named(packed, number // 4), named(usual, number - number // 4 - 1))
    mixed = jax.random.permutation(jax.random.fold_in(own, 3), count)
    source_of, receiver = mixed[0:count // 2 * 2:2], mixed[1:count // 2 * 2:2]
    margin = jnp.minimum(tallies[source_of] - 1, most - tallies[receiver]) // 2
    margin = jnp.where((source_of == ranking[0]) | (receiver == ranking[0]) | (tallies[receiver] == 0), 0, jnp.maximum(margin, 0))
    moved = jax.random.randint(jax.random.fold_in(own, 4), (count // 2,), 0, 1 << 20) % (margin + 1)
    tallies = tallies.at[source_of].add(-moved).at[receiver].add(moved)
    items = jnp.searchsorted(jnp.cumsum(tallies), jnp.arange(rows * top), side="right").astype(jnp.int32)
    grid = items.reshape(top, rows).T
    grid = grid[jax.random.permutation(jax.random.fold_in(own, 1), rows)]
    rotation = jax.random.randint(jax.random.fold_in(own, 2), (rows, 1), 0, top)
    return jnp.take_along_axis(grid, (jnp.arange(top)[None, :] + rotation) % top, axis=1)


def shares(count, total, reach, slope, full):
    weights = [(1 << 20) // math.isqrt(standing ** slope) + 1 for standing in range(1, count + 1)]
    largest = reach if full else min(reach, max(-(-total // count), total * weights[0] // sum(weights)))
    least = 1 if total - largest >= count - 1 else 0
    given, rest = [largest] + [least] * (count - 1), total - largest - least * (count - 1)
    while rest > 0:
        candidates = [i for i in range(1, count) if given[i] < largest] or [i for i in range(1, count) if given[i] < reach]
        pool, left = sum([weights[i] for i in candidates]), rest
        for i in candidates:
            more = min(reach - given[i], max(1, left * weights[i] // pool), rest)
            given[i] = given[i] + more
            rest = rest - more
    return np.array(given)


def normal_values(stream_key, dims, scale, most, split=(), held_as=jnp.bfloat16):
    values = scale * jax.random.normal(stream_key, dims, jnp.float32)
    if split:
        values = values * shard_levels(stream_key, dims, split, -0.22, 0.18)
    return jnp.clip(values, -most, most).astype(held_as)


def setup_inputs(seed: int = 0) -> dict:
    key_of = jax.random.split(jax.random.key(seed), 6)
    voltages = normal_values(key_of[0], (STATIONS, CHANNELS, 2 * SAMPLES), 1.0, 6.0, ((0, 16), (1, 32)))
    block_facet_keys = jax.random.split(jax.random.fold_in(key_of[1], 1), CGROUPS * FACETS * BLK_DEV // BLK_DEV)
    block_facet_turns = jax.random.permutation(jax.random.fold_in(key_of[1], 3), CGROUPS * FACETS * BLK_DEV // BLK_DEV)
    block_facet = jax.vmap(lambda own, number: deal_out(jax.random.fold_in(key_of[1], 2), own, number, BLK_DEV, FACETS, 1, CAP, 2))(block_facet_keys, block_facet_turns).reshape((CGROUPS, FACETS, BLK_DEV, 1))
    block_tile = with_ends(jax.random.randint(key_of[2], (CGROUPS, FACETS, BLK_DEV), 0, TT), jax.random.fold_in(key_of[2], 1), 0, TT - 1).astype(jnp.int32)
    vis_offset = with_ends(jax.random.randint(key_of[3], (CGROUPS, FACETS, BLK_DEV, VB), 0, OFFS * OFFS), jax.random.fold_in(key_of[3], 1), 0, (OFFS * OFFS) - 1).astype(jnp.int32)
    kernel_taps = jnp.clip(jax.random.uniform(key_of[4], (2, KT), jnp.float32, 0.19921875, 1.0), 0.19921875, 1.0).astype(jnp.bfloat16)
    return dict(voltages=voltages, block_facet=block_facet, block_tile=block_tile, vis_offset=vis_offset, kernel_taps=kernel_taps)


def kernel_rows(offsets, taps_row):
    cell_ids = jnp.arange(TILE, dtype=jnp.int32)
    distance = cell_ids[None, :, None] - offsets[:, None, :]
    weights_sum = jnp.zeros(distance.shape, jnp.float32)
    for tap_index in range(KT):
        weights_sum = weights_sum + jnp.where(distance == tap_index, taps_row[tap_index].astype(jnp.float32), jnp.float32(0.0))
    return weights_sum.astype(jnp.bfloat16)

def block_tiles(values, offsets, kernel_taps):
    along_u = kernel_rows(offsets // OFFS, kernel_taps[0])
    along_v = kernel_rows(offsets % OFFS, kernel_taps[1])
    weighted = (values[:, :, None, :].astype(jnp.float32) * along_v[:, None, :, :].astype(jnp.float32)).astype(jnp.bfloat16)
    weighted = weighted.reshape(values.shape[0], 2 * TILE, values.shape[2])
    return jnp.einsum('nux,nwx->nuw', along_u.astype(jnp.float32), weighted.astype(jnp.float32))

def reference(voltages, block_facet, block_tile, vis_offset, kernel_taps):
    per_channel = STATIONS * STATIONS // VB
    by_channel = jnp.transpose(voltages, (1, 0, 2))
    facet_rows = block_facet.reshape(CHANNELS, per_channel)
    tile_rows = block_tile.reshape(CHANNELS, per_channel)
    offset_rows = vis_offset.reshape(CHANNELS, per_channel, VB)
    station_ids = jnp.arange(STATIONS, dtype=jnp.int32)
    off_diagonal = (station_ids[:, None] != station_ids[None, :]).astype(jnp.float32)
    scale = 1.0 / math.sqrt(SAMPLES)

    def one_channel(grids, inputs):
        panel, facets_here, tiles_here, offsets_here = inputs
        whole = panel.astype(jnp.float32)
        swapped = jnp.concatenate([whole[:, SAMPLES:], -whole[:, :SAMPLES]], axis=1)
        real_vis = (jnp.dot(whole, whole.T, preferred_element_type=jnp.float32) * scale * off_diagonal).astype(jnp.bfloat16)
        imag_vis = (jnp.dot(swapped, whole.T, preferred_element_type=jnp.float32) * scale * off_diagonal).astype(jnp.bfloat16)
        values = jnp.stack([real_vis.reshape(per_channel, VB), imag_vis.reshape(per_channel, VB)], axis=1)
        tile_sums = block_tiles(values, offsets_here, kernel_taps).reshape(per_channel, 2 * TILE * TILE)
        targets = (facets_here * TT + tiles_here).astype(jnp.int32)
        return (grids + jax.ops.segment_sum(tile_sums, targets, num_segments=FACETS * TT), None)
    start_grids = jnp.zeros((FACETS * TT, 2 * TILE * TILE), jnp.float32)
    grids, leftover = lax.scan(one_channel, start_grids, (by_channel, facet_rows, tile_rows, offset_rows))
    shaped = grids.reshape(FACETS, TS, TS, TILE, 2, TILE)
    planes = jnp.transpose(shaped, (0, 4, 1, 3, 2, 5)).reshape(FACETS, 2, FG, FG)
    spectrum = jnp.fft.fft2(planes[:, 0] + 1j * planes[:, 1])
    norm_factor = 1.0 / math.sqrt(CHANNELS * STATIONS * STATIONS * KT * KT / FACETS)
    image = jnp.stack([jnp.real(spectrum), jnp.imag(spectrum)], axis=0) * norm_factor
    return image.reshape(2, FACETS * FG, FG).astype(jnp.float32)
```

```python
import functools
import math

import jax
import jax.numpy as jnp
from jax import lax
from jax.experimental import pallas as pl
from jax.experimental.pallas import tpu as pltpu
from jax.sharding import PartitionSpec as P

VB = 128
TILE = 32
KT = 8
TS = 4
TT = 16
OFFS = 25
CHUNK = 256


def grid_kernel(seg_ref, du_ref, dv_ref, re_ref, im_ref, out_ref):
    step = pl.program_id(0)

    @pl.when(step == 0)
    def _():
        out_ref[...] = jnp.zeros_like(out_ref)

    cells = lax.broadcasted_iota(jnp.int32, (TILE, VB), 0)

    def one_block(b, carry):
        du = du_ref[pl.ds(b, 1), :]
        dv = dv_ref[pl.ds(b, 1), :]
        re = re_ref[pl.ds(b, 1), :]
        im = im_ref[pl.ds(b, 1), :]
        along_u = (cells == du).astype(jnp.float32).astype(jnp.bfloat16)
        hit_v = cells == dv
        weighted = jnp.concatenate(
            [jnp.where(hit_v, re, 0.0), jnp.where(hit_v, im, 0.0)], axis=0
        ).astype(jnp.bfloat16)
        tile_sum = lax.dot_general(
            along_u, weighted, (((1,), (1,)), ((), ())), preferred_element_type=jnp.float32
        )
        seg = seg_ref[step * CHUNK + b]
        out_ref[seg] += tile_sum
        return carry

    lax.fori_loop(0, CHUNK, one_block, 0, unroll=8)


def grid_blocks(seg_ids, du, dv, re, im, segments):
    blocks = du.shape[0]
    row_spec = pl.BlockSpec((CHUNK, VB), lambda i, seg: (i, 0))
    return pl.pallas_call(
        grid_kernel,
        out_shape=jax.ShapeDtypeStruct((segments, TILE, 2 * TILE), jnp.float32),
        grid_spec=pltpu.PrefetchScalarGridSpec(
            num_scalar_prefetch=1,
            grid=(blocks // CHUNK,),
            in_specs=[row_spec] * 4,
            out_specs=pl.BlockSpec((segments, TILE, 2 * TILE), lambda i, seg: (0, 0, 0)),
        ),
        cost_estimate=pl.CostEstimate(
            flops=blocks * TILE * VB * 2 * TILE * 2,
            bytes_accessed=blocks * VB * 16 + segments * TILE * 2 * TILE * 4,
            transcendentals=0,
        ),
    )(seg_ids, du, dv, re, im)


def dft_tables(side):
    index_ids = jnp.arange(side, dtype=jnp.int32)
    phases = index_ids[:, None] * index_ids[None, :] % side
    angles = phases.astype(jnp.float32) * (2.0 * math.pi / side)
    return (jnp.cos(angles), jnp.sin(angles))


def taps_transform(taps_row, side):
    index_ids = jnp.arange(side, dtype=jnp.int32)
    tap_ids = jnp.arange(KT, dtype=jnp.int32)
    phases = index_ids[:, None] * tap_ids[None, :] % side
    angles = phases.astype(jnp.float32) * (2.0 * math.pi / side)
    taps = taps_row.astype(jnp.float32)
    return (jnp.sum(jnp.cos(angles) * taps, axis=1), -jnp.sum(jnp.sin(angles) * taps, axis=1))


def body(voltages, block_facet, block_tile, vis_offset, kernel_taps):
    facets = lax.axis_size("stn")
    chan_count = lax.axis_size("chan")
    high = lax.Precision.HIGHEST
    panels = lax.all_to_all(voltages, "stn", split_axis=1, concat_axis=0, tiled=True)
    stations = panels.shape[0]
    local_channels = panels.shape[1]
    samples = panels.shape[2] // 2
    swapped = jnp.concatenate([panels[:, :, samples:], -panels[:, :, :samples]], axis=2)
    stacked = jnp.concatenate([panels, swapped], axis=0)
    products = jnp.einsum("aks,jks->kaj", stacked, panels, preferred_element_type=jnp.float32)
    station_ids = jnp.arange(stations, dtype=jnp.int32)
    off_diagonal = (station_ids[:, None] != station_ids[None, :]).astype(jnp.float32)
    scale = 1.0 / math.sqrt(samples)
    real_vis = (products[:, :stations, :] * scale * off_diagonal).astype(jnp.bfloat16)
    imag_vis = (products[:, stations:, :] * scale * off_diagonal).astype(jnp.bfloat16)
    re = real_vis.reshape(-1, VB).astype(jnp.float32)
    im = imag_vis.reshape(-1, VB).astype(jnp.float32)
    block_count = re.shape[0]
    offsets = vis_offset.reshape(block_count, VB)
    du = offsets // OFFS
    dv = offsets % OFFS
    seg_ids = block_facet.reshape(block_count) * TT + block_tile.reshape(block_count)
    tiles = grid_blocks(seg_ids, du, dv, re, im, facets * TT)
    side = TS * TILE
    delta = tiles.reshape(facets, TS, TS, TILE, 2, TILE)
    delta = jnp.transpose(delta, (0, 4, 1, 3, 2, 5)).reshape(facets, 2, side, side)
    cosine, sine = dft_tables(side)
    along_x = jnp.stack(
        [jnp.stack([cosine, sine], axis=1), jnp.stack([-sine, cosine], axis=1)], axis=1
    )
    rows = jnp.einsum("xqpu,fpuv->fxqv", along_x, delta, precision=high)
    rows = rows.reshape(facets * side, 2, side)
    mine = lax.psum_scatter(rows, ("stn", "chan"), scatter_dimension=0, tiled=True)
    row_count = mine.shape[0]
    along_y = jnp.stack(
        [jnp.stack([cosine, -sine], axis=1), jnp.stack([sine, cosine], axis=1)], axis=0
    )
    spectrum = jnp.einsum("rqv,qvsy->rsy", mine, along_y, precision=high)
    first_row = lax.axis_index("chan") * row_count
    u_re, u_im = taps_transform(kernel_taps[0], side)
    v_re, v_im = taps_transform(kernel_taps[1], side)
    u_re = lax.dynamic_slice_in_dim(u_re, first_row, row_count, 0)[:, None]
    u_im = lax.dynamic_slice_in_dim(u_im, first_row, row_count, 0)[:, None]
    k_re = u_re * v_re[None, :] - u_im * v_im[None, :]
    k_im = u_re * v_im[None, :] + u_im * v_re[None, :]
    s_re = spectrum[:, 0, :]
    s_im = spectrum[:, 1, :]
    channels_all = local_channels * facets * chan_count
    norm_factor = 1.0 / math.sqrt(channels_all * stations * stations * KT * KT / facets)
    image_re = (s_re * k_re - s_im * k_im) * norm_factor
    image_im = (s_re * k_im + s_im * k_re) * norm_factor
    return jnp.stack([image_re, image_im], axis=0)


def solution(mesh):
    placed = (
        P("stn", "chan", None),
        P("chan", "stn", None, None),
        P("chan", "stn", None),
        P("chan", "stn", None, None),
        P(),
    )
    return jax.shard_map(
        body, mesh=mesh, in_specs=placed, out_specs=P(None, ("stn", "chan"), None), check_vma=False
    )
```

```python
import functools
import math

import jax
import jax.numpy as jnp
from jax import lax
from jax.experimental import pallas as pl
from jax.experimental.pallas import tpu as pltpu
from jax.sharding import PartitionSpec as P

VB = 128
TILE = 32
KT = 8
TS = 4
TT = 16
OFFS = 25
CHUNK = 256


def grid_kernel(seg_ref, du_ref, dv_ref, re_ref, im_ref, out_ref):
    step = pl.program_id(0)

    @pl.when(step == 0)
    def _():
        out_ref[...] = jnp.zeros_like(out_ref)

    cells = lax.broadcasted_iota(jnp.int32, (TILE, VB), 0)

    def one_block(b, carry):
        du = du_ref[pl.ds(b, 1), :]
        dv = dv_ref[pl.ds(b, 1), :]
        re = re_ref[pl.ds(b, 1), :]
        im = im_ref[pl.ds(b, 1), :]
        along_u = (cells == du).astype(jnp.float32).astype(jnp.bfloat16)
        hit_v = cells == dv
        weighted = jnp.concatenate(
            [jnp.where(hit_v, re, 0.0), jnp.where(hit_v, im, 0.0)], axis=0
        ).astype(jnp.bfloat16)
        tile_sum = lax.dot_general(
            along_u, weighted, (((1,), (1,)), ((), ())), preferred_element_type=jnp.float32
        )
        seg = seg_ref[step * CHUNK + b]
        out_ref[seg] += tile_sum
        return carry

    lax.fori_loop(0, CHUNK, one_block, 0, unroll=8)


def grid_blocks(seg_ids, du, dv, re, im, segments):
    blocks = du.shape[0]
    row_spec = pl.BlockSpec((CHUNK, VB), lambda i, seg: (i, 0))
    return pl.pallas_call(
        grid_kernel,
        out_shape=jax.ShapeDtypeStruct((segments, TILE, 2 * TILE), jnp.float32),
        grid_spec=pltpu.PrefetchScalarGridSpec(
            num_scalar_prefetch=1,
            grid=(blocks // CHUNK,),
            in_specs=[row_spec] * 4,
            out_specs=pl.BlockSpec((segments, TILE, 2 * TILE), lambda i, seg: (0, 0, 0)),
        ),
        cost_estimate=pl.CostEstimate(
            flops=blocks * TILE * VB * 2 * TILE * 2,
            bytes_accessed=blocks * VB * 16 + segments * TILE * 2 * TILE * 4,
            transcendentals=0,
        ),
    )(seg_ids, du, dv, re, im)


def dft_tables(side):
    index_ids = jnp.arange(side, dtype=jnp.int32)
    phases = index_ids[:, None] * index_ids[None, :] % side
    angles = phases.astype(jnp.float32) * (2.0 * math.pi / side)
    return (jnp.cos(angles), jnp.sin(angles))


def taps_transform(taps_row, side):
    index_ids = jnp.arange(side, dtype=jnp.int32)
    tap_ids = jnp.arange(KT, dtype=jnp.int32)
    phases = index_ids[:, None] * tap_ids[None, :] % side
    angles = phases.astype(jnp.float32) * (2.0 * math.pi / side)
    taps = taps_row.astype(jnp.float32)
    return (jnp.sum(jnp.cos(angles) * taps, axis=1), -jnp.sum(jnp.sin(angles) * taps, axis=1))


def body(voltages, block_facet, block_tile, vis_offset, kernel_taps):
    facets = lax.axis_size("stn")
    chan_count = lax.axis_size("chan")
    high = lax.Precision.HIGHEST
    panels = lax.all_to_all(voltages, "stn", split_axis=1, concat_axis=0, tiled=True)
    stations = panels.shape[0]
    local_channels = panels.shape[1]
    samples = panels.shape[2] // 2
    swapped = jnp.concatenate([panels[:, :, samples:], -panels[:, :, :samples]], axis=2)
    stacked = jnp.concatenate([panels, swapped], axis=0)
    products = jnp.einsum("aks,jks->kaj", stacked, panels, preferred_element_type=jnp.float32)
    station_ids = jnp.arange(stations, dtype=jnp.int32)
    off_diagonal = (station_ids[:, None] != station_ids[None, :]).astype(jnp.float32)
    scale = 1.0 / math.sqrt(samples)
    real_vis = (products[:, :stations, :] * scale * off_diagonal).astype(jnp.bfloat16)
    imag_vis = (products[:, stations:, :] * scale * off_diagonal).astype(jnp.bfloat16)
    re = real_vis.reshape(-1, VB).astype(jnp.float32)
    im = imag_vis.reshape(-1, VB).astype(jnp.float32)
    block_count = re.shape[0]
    offsets = vis_offset.reshape(block_count, VB)
    du = offsets // OFFS
    dv = offsets % OFFS
    seg_ids = block_facet.reshape(block_count) * TT + block_tile.reshape(block_count)
    tiles = grid_blocks(seg_ids, du, dv, re, im, facets * TT)
    side = TS * TILE
    delta = tiles.reshape(facets, TS, TS, TILE, 2, TILE)
    delta = delta[..., :OFFS]
    delta = jnp.transpose(delta, (0, 4, 1, 3, 2, 5)).reshape(facets, 2, side, TS * OFFS)
    cosine, sine = dft_tables(side)
    along_x = jnp.stack(
        [jnp.stack([cosine, sine], axis=1), jnp.stack([-sine, cosine], axis=1)], axis=1
    )
    rows = jnp.einsum("xqpu,fpuv->fxqv", along_x, delta, precision=high)
    row_count = side // chan_count
    rows = rows.reshape(facets, chan_count, row_count, 2, TS * OFFS)
    rows = jnp.transpose(rows, (1, 0, 2, 3, 4)).reshape(chan_count * facets * row_count, 2, TS * OFFS)
    rows = lax.psum_scatter(rows, "chan", scatter_dimension=0, tiled=True)
    mine = lax.psum_scatter(rows, "stn", scatter_dimension=0, tiled=True)
    used = jnp.arange(TS * OFFS, dtype=jnp.int32)
    used = (used // OFFS) * TILE + used % OFFS
    cos_used = cosine[used]
    sin_used = sine[used]
    along_y = jnp.stack(
        [jnp.stack([cos_used, -sin_used], axis=1), jnp.stack([sin_used, cos_used], axis=1)], axis=0
    )
    spectrum = jnp.einsum("rqv,qvsy->rsy", mine, along_y, precision=high)
    first_row = lax.axis_index("chan") * row_count
    u_re, u_im = taps_transform(kernel_taps[0], side)
    v_re, v_im = taps_transform(kernel_taps[1], side)
    u_re = lax.dynamic_slice_in_dim(u_re, first_row, row_count, 0)[:, None]
    u_im = lax.dynamic_slice_in_dim(u_im, first_row, row_count, 0)[:, None]
    k_re = u_re * v_re[None, :] - u_im * v_im[None, :]
    k_im = u_re * v_im[None, :] + u_im * v_re[None, :]
    s_re = spectrum[:, 0, :]
    s_im = spectrum[:, 1, :]
    channels_all = local_channels * facets * chan_count
    norm_factor = 1.0 / math.sqrt(channels_all * stations * stations * KT * KT / facets)
    image_re = (s_re * k_re - s_im * k_im) * norm_factor
    image_im = (s_re * k_im + s_im * k_re) * norm_factor
    return jnp.stack([image_re, image_im], axis=0)


def solution(mesh):
    placed = (
        P("stn", "chan", None),
        P("chan", "stn", None, None),
        P("chan", "stn", None),
        P("chan", "stn", None, None),
        P(),
    )
    return jax.shard_map(
        body, mesh=mesh, in_specs=placed, out_specs=P(None, ("stn", "chan"), None), check_vma=False
    )
```

```python
import functools
import math

import jax
import jax.numpy as jnp
from jax import lax
from jax.experimental import pallas as pl
from jax.experimental.pallas import tpu as pltpu
from jax.sharding import PartitionSpec as P

VB = 128
TILE = 32
KT = 8
TS = 4
TT = 16
OFFS = 25
CHUNK = 256


def grid_kernel(seg_ref, du_ref, dv_ref, re_ref, im_ref, out_ref):
    step = pl.program_id(0)

    @pl.when(step == 0)
    def _():
        out_ref[...] = jnp.zeros_like(out_ref)

    cells = lax.broadcasted_iota(jnp.int32, (TILE, VB), 0)

    def one_block(b, carry):
        du = du_ref[pl.ds(b, 1), :]
        dv = dv_ref[pl.ds(b, 1), :]
        re = re_ref[pl.ds(b, 1), :]
        im = im_ref[pl.ds(b, 1), :]
        along_u = (cells == du).astype(jnp.float32).astype(jnp.bfloat16)
        hit_v = cells == dv
        weighted = jnp.concatenate(
            [jnp.where(hit_v, re, 0.0), jnp.where(hit_v, im, 0.0)], axis=0
        ).astype(jnp.bfloat16)
        tile_sum = lax.dot_general(
            along_u, weighted, (((1,), (1,)), ((), ())), preferred_element_type=jnp.float32
        )
        seg = seg_ref[step * CHUNK + b]
        out_ref[seg] += tile_sum
        return carry

    lax.fori_loop(0, CHUNK, one_block, 0, unroll=8)


def grid_blocks(seg_ids, du, dv, re, im, segments):
    blocks = du.shape[0]
    row_spec = pl.BlockSpec((CHUNK, VB), lambda i, seg: (i, 0))
    return pl.pallas_call(
        grid_kernel,
        out_shape=jax.ShapeDtypeStruct((segments, TILE, 2 * TILE), jnp.float32),
        grid_spec=pltpu.PrefetchScalarGridSpec(
            num_scalar_prefetch=1,
            grid=(blocks // CHUNK,),
            in_specs=[row_spec] * 4,
            out_specs=pl.BlockSpec((segments, TILE, 2 * TILE), lambda i, seg: (0, 0, 0)),
        ),
        cost_estimate=pl.CostEstimate(
            flops=blocks * TILE * VB * 2 * TILE * 2,
            bytes_accessed=blocks * VB * 16 + segments * TILE * 2 * TILE * 4,
            transcendentals=0,
        ),
    )(seg_ids, du, dv, re, im)


def dft_tables(side):
    index_ids = jnp.arange(side, dtype=jnp.int32)
    phases = index_ids[:, None] * index_ids[None, :] % side
    angles = phases.astype(jnp.float32) * (2.0 * math.pi / side)
    return (jnp.cos(angles), jnp.sin(angles))


def taps_transform(taps_row, side):
    index_ids = jnp.arange(side, dtype=jnp.int32)
    tap_ids = jnp.arange(KT, dtype=jnp.int32)
    phases = index_ids[:, None] * tap_ids[None, :] % side
    angles = phases.astype(jnp.float32) * (2.0 * math.pi / side)
    taps = taps_row.astype(jnp.float32)
    return (jnp.sum(jnp.cos(angles) * taps, axis=1), -jnp.sum(jnp.sin(angles) * taps, axis=1))


def body(voltages, block_facet, block_tile, vis_offset, kernel_taps):
    facets = lax.axis_size("stn")
    chan_count = lax.axis_size("chan")
    high = lax.Precision.HIGHEST
    panels = lax.all_to_all(voltages, "stn", split_axis=1, concat_axis=0, tiled=True)
    stations = panels.shape[0]
    local_channels = panels.shape[1]
    samples = panels.shape[2] // 2
    swapped = jnp.concatenate([panels[:, :, samples:], -panels[:, :, :samples]], axis=2)
    stacked = jnp.concatenate([panels, swapped], axis=0)
    products = jnp.einsum("aks,jks->kaj", stacked, panels, preferred_element_type=jnp.float32)
    station_ids = jnp.arange(stations, dtype=jnp.int32)
    off_diagonal = (station_ids[:, None] != station_ids[None, :]).astype(jnp.float32)
    scale = 1.0 / math.sqrt(samples)
    real_vis = (products[:, :stations, :] * scale * off_diagonal).astype(jnp.bfloat16)
    imag_vis = (products[:, stations:, :] * scale * off_diagonal).astype(jnp.bfloat16)
    re = real_vis.reshape(-1, VB).astype(jnp.float32)
    im = imag_vis.reshape(-1, VB).astype(jnp.float32)
    block_count = re.shape[0]
    offsets = vis_offset.reshape(block_count, VB)
    du = offsets // OFFS
    dv = offsets % OFFS
    seg_ids = block_facet.reshape(block_count) * TT + block_tile.reshape(block_count)
    tiles = grid_blocks(seg_ids, du, dv, re, im, facets * TT)
    side = TS * TILE
    delta = tiles.reshape(facets, TS, TS, TILE, 2, TILE)
    delta = delta[..., :OFFS]
    delta = jnp.transpose(delta, (0, 4, 1, 3, 2, 5)).reshape(facets, 2, side, TS * OFFS)
    cosine, sine = dft_tables(side)
    along_x = jnp.stack(
        [jnp.stack([cosine, sine], axis=1), jnp.stack([-sine, cosine], axis=1)], axis=1
    )
    rows = jnp.einsum("xqpu,fpuv->fxqv", along_x, delta, precision=high)
    row_count = side // chan_count
    rows = rows.reshape(facets, chan_count, row_count, 2, TS * OFFS)
    rows = jnp.transpose(rows, (1, 0, 2, 3, 4)).reshape(chan_count * facets * row_count, 2, TS * OFFS)
    rows = lax.all_to_all(rows, "chan", split_axis=0, concat_axis=0, tiled=True)
    rows = jnp.sum(rows.reshape(chan_count, facets * row_count, 2, TS * OFFS), axis=0)
    rows = lax.all_to_all(rows, "stn", split_axis=0, concat_axis=0, tiled=True)
    mine = jnp.sum(rows.reshape(facets, row_count, 2, TS * OFFS), axis=0)
    used = jnp.arange(TS * OFFS, dtype=jnp.int32)
    used = (used // OFFS) * TILE + used % OFFS
    cos_used = cosine[used]
    sin_used = sine[used]
    along_y = jnp.stack(
        [jnp.stack([cos_used, -sin_used], axis=1), jnp.stack([sin_used, cos_used], axis=1)], axis=0
    )
    spectrum = jnp.einsum("rqv,qvsy->rsy", mine, along_y, precision=high)
    first_row = lax.axis_index("chan") * row_count
    u_re, u_im = taps_transform(kernel_taps[0], side)
    v_re, v_im = taps_transform(kernel_taps[1], side)
    u_re = lax.dynamic_slice_in_dim(u_re, first_row, row_count, 0)[:, None]
    u_im = lax.dynamic_slice_in_dim(u_im, first_row, row_count, 0)[:, None]
    k_re = u_re * v_re[None, :] - u_im * v_im[None, :]
    k_im = u_re * v_im[None, :] + u_im * v_re[None, :]
    s_re = spectrum[:, 0, :]
    s_im = spectrum[:, 1, :]
    channels_all = local_channels * facets * chan_count
    norm_factor = 1.0 / math.sqrt(channels_all * stations * stations * KT * KT / facets)
    image_re = (s_re * k_re - s_im * k_im) * norm_factor
    image_im = (s_re * k_im + s_im * k_re) * norm_factor
    return jnp.stack([image_re, image_im], axis=0)


def solution(mesh):
    placed = (
        P("stn", "chan", None),
        P("chan", "stn", None, None),
        P("chan", "stn", None),
        P("chan", "stn", None, None),
        P(),
    )
    return jax.shard_map(
        body, mesh=mesh, in_specs=placed, out_specs=P(None, ("stn", "chan"), None), check_vma=False
    )
```

```python
import functools
import math

import jax
import jax.numpy as jnp
from jax import lax
from jax.experimental import pallas as pl
from jax.experimental.pallas import tpu as pltpu
from jax.sharding import PartitionSpec as P

VB = 128
TILE = 32
KT = 8
TS = 4
TT = 16
OFFS = 25
CHUNK = 256


def grid_kernel(seg_ref, du_ref, dv_ref, re_ref, im_ref, out_ref):
    step = pl.program_id(0)
    side = TS * TILE

    @pl.when(step == 0)
    def _():
        out_ref[...] = jnp.zeros_like(out_ref)
    cells = lax.broadcasted_iota(jnp.int32, (TILE, VB), 0)
    lines = lax.broadcasted_iota(jnp.int32, (side, VB), 0)
    def one_block(b, carry):
        du = du_ref[pl.ds(b, 1), :]
        dv = dv_ref[pl.ds(b, 1), :]
        re = re_ref[pl.ds(b, 1), :]
        im = im_ref[pl.ds(b, 1), :]
        seg = seg_ref[step * CHUNK + b]
        facet = seg // TT
        tile = seg % TT
        first_u = pl.multiple_of((tile // TS) * TILE, TILE)
        first_v = (tile % TS) * TILE
        along_u = (cells == du).astype(jnp.float32).astype(jnp.bfloat16)
        hit_v = lines == (dv + first_v)
        spread = jnp.concatenate(
            [jnp.where(hit_v, re, 0.0), jnp.where(hit_v, im, 0.0)], axis=0
        ).astype(jnp.bfloat16)
        tile_sum = lax.dot_general(
            along_u, spread, (((1,), (1,)), ((), ())), preferred_element_type=jnp.float32
        )
        out_ref[facet, pl.ds(first_u, TILE), :] += tile_sum
        return carry
    lax.fori_loop(0, CHUNK, one_block, 0, unroll=8)


def grid_blocks(seg_ids, du, dv, re, im, facets):
    blocks = du.shape[0]
    side = TS * TILE
    row_spec = pl.BlockSpec((CHUNK, VB), lambda i, seg: (i, 0))
    return pl.pallas_call(
        grid_kernel,
        out_shape=jax.ShapeDtypeStruct((facets, side, 2 * side), jnp.float32),
        grid_spec=pltpu.PrefetchScalarGridSpec(
            num_scalar_prefetch=1,
            grid=(blocks // CHUNK,),
            in_specs=[row_spec] * 4,
            out_specs=pl.BlockSpec((facets, side, 2 * side), lambda i, seg: (0, 0, 0)),
        ),
        cost_estimate=pl.CostEstimate(
            flops=blocks * TILE * VB * 2 * side * 2,
            bytes_accessed=blocks * VB * 16 + facets * side * 2 * side * 4,
            transcendentals=0,
        ),
    )(seg_ids, du, dv, re, im)


def dft_tables(side):
    index_ids = jnp.arange(side, dtype=jnp.int32)
    phases = index_ids[:, None] * index_ids[None, :] % side
    angles = phases.astype(jnp.float32) * (2.0 * math.pi / side)
    return (jnp.cos(angles), jnp.sin(angles))


def taps_transform(taps_row, side):
    index_ids = jnp.arange(side, dtype=jnp.int32)
    tap_ids = jnp.arange(KT, dtype=jnp.int32)
    phases = index_ids[:, None] * tap_ids[None, :] % side
    angles = phases.astype(jnp.float32) * (2.0 * math.pi / side)
    taps = taps_row.astype(jnp.float32)
    return (jnp.sum(jnp.cos(angles) * taps, axis=1), -jnp.sum(jnp.sin(angles) * taps, axis=1))


def body(voltages, block_facet, block_tile, vis_offset, kernel_taps):
    facets = lax.axis_size("stn")
    chan_count = lax.axis_size("chan")
    high = lax.Precision.HIGHEST
    panels = lax.all_to_all(voltages, "stn", split_axis=1, concat_axis=0, tiled=True)
    stations = panels.shape[0]
    local_channels = panels.shape[1]
    samples = panels.shape[2] // 2
    swapped = jnp.concatenate([panels[:, :, samples:], -panels[:, :, :samples]], axis=2)
    stacked = jnp.concatenate([panels, swapped], axis=0)
    products = jnp.einsum("aks,jks->kaj", stacked, panels, preferred_element_type=jnp.float32)
    station_ids = jnp.arange(stations, dtype=jnp.int32)
    off_diagonal = (station_ids[:, None] != station_ids[None, :]).astype(jnp.float32)
    scale = 1.0 / math.sqrt(samples)
    real_vis = (products[:, :stations, :] * scale * off_diagonal).astype(jnp.bfloat16)
    imag_vis = (products[:, stations:, :] * scale * off_diagonal).astype(jnp.bfloat16)
    re = real_vis.reshape(-1, VB).astype(jnp.float32)
    im = imag_vis.reshape(-1, VB).astype(jnp.float32)
    block_count = re.shape[0]
    offsets = vis_offset.reshape(block_count, VB)
    du = offsets // OFFS
    dv = offsets % OFFS
    seg_ids = block_facet.reshape(block_count) * TT + block_tile.reshape(block_count)
    delta = grid_blocks(seg_ids, du, dv, re, im, facets)
    side = TS * TILE
    row_count = side // chan_count
    cosine, sine = dft_tables(side)
    along_x = jnp.stack(
        [jnp.stack([cosine, sine], axis=2), jnp.stack([-sine, cosine], axis=2)], axis=1
    ).reshape(2 * side, 2 * side)
    rows = jnp.einsum("kc,fcv->kfv", along_x, delta.reshape(facets, 2 * side, side), precision=high)
    rows = rows.reshape(chan_count * row_count * 2 * facets, side)
    rows = lax.all_to_all(rows, "chan", split_axis=0, concat_axis=0, tiled=True)
    rows = jnp.sum(rows.reshape(chan_count, row_count * 2, facets, side), axis=0)
    rows = jnp.transpose(rows, (1, 0, 2)).reshape(facets * row_count * 2, side)
    rows = lax.all_to_all(rows, "stn", split_axis=0, concat_axis=0, tiled=True)
    mine = jnp.sum(rows.reshape(facets, row_count, 2, side), axis=0)
    along_y = jnp.stack(
        [jnp.stack([cosine, -sine], axis=1), jnp.stack([sine, cosine], axis=1)], axis=0
    )
    spectrum = jnp.einsum("rqv,qvsy->rsy", mine, along_y, precision=high)
    first_row = lax.axis_index("chan") * row_count
    u_re, u_im = taps_transform(kernel_taps[0], side)
    v_re, v_im = taps_transform(kernel_taps[1], side)
    u_re = lax.dynamic_slice_in_dim(u_re, first_row, row_count, 0)[:, None]
    u_im = lax.dynamic_slice_in_dim(u_im, first_row, row_count, 0)[:, None]
    k_re = u_re * v_re[None, :] - u_im * v_im[None, :]
    k_im = u_re * v_im[None, :] + u_im * v_re[None, :]
    s_re = spectrum[:, 0, :]
    s_im = spectrum[:, 1, :]
    channels_all = local_channels * facets * chan_count
    norm_factor = 1.0 / math.sqrt(channels_all * stations * stations * KT * KT / facets)
    image_re = (s_re * k_re - s_im * k_im) * norm_factor
    image_im = (s_re * k_im + s_im * k_re) * norm_factor
    return jnp.stack([image_re, image_im], axis=0)


def solution(mesh):
    placed = (
        P("stn", "chan", None),
        P("chan", "stn", None, None),
        P("chan", "stn", None),
        P("chan", "stn", None, None),
        P(),
    )
    return jax.shard_map(
        body, mesh=mesh, in_specs=placed, out_specs=P(None, ("stn", "chan"), None), check_vma=False
    )
```

```python
import functools
import math

import jax
import jax.numpy as jnp
from jax import lax
from jax.experimental import pallas as pl
from jax.experimental.pallas import tpu as pltpu
from jax.sharding import PartitionSpec as P

VB = 128
TILE = 32
KT = 8
TS = 4
TT = 16
OFFS = 25
CHUNK = 256


def grid_kernel(seg_ref, du_ref, dv_ref, re_ref, im_ref, out_ref):
    step = pl.program_id(0)
    side = TS * TILE

    @pl.when(step == 0)
    def _():
        out_ref[...] = jnp.zeros_like(out_ref)
    cells = lax.broadcasted_iota(jnp.int32, (TILE, VB), 0)
    def one_block(b, carry):
        du = du_ref[pl.ds(b, 1), :]
        dv = dv_ref[pl.ds(b, 1), :]
        re = re_ref[pl.ds(b, 1), :]
        im = im_ref[pl.ds(b, 1), :]
        seg = seg_ref[step * CHUNK + b]
        facet = seg // TT
        tile = seg % TT
        first_u = pl.multiple_of((tile // TS) * TILE, TILE)
        tile_v = tile % TS
        along_u = (cells == du).astype(jnp.float32).astype(jnp.bfloat16)
        hit_v = cells == dv
        parts = [jnp.where(hit_v, re, 0.0).astype(jnp.bfloat16), jnp.where(hit_v, im, 0.0).astype(jnp.bfloat16)]
        empty = jnp.zeros((TILE, VB), jnp.bfloat16)
        spread = jnp.concatenate(
            [jnp.where(tile_v == t, part, empty) for part in parts for t in range(TS)], axis=0
        )
        tile_sum = lax.dot_general(
            along_u, spread, (((1,), (1,)), ((), ())), preferred_element_type=jnp.float32
        )
        out_ref[facet, pl.ds(first_u, TILE), :] += tile_sum
        return carry
    lax.fori_loop(0, CHUNK, one_block, 0, unroll=8)


def grid_blocks(seg_ids, du, dv, re, im, facets):
    blocks = du.shape[0]
    side = TS * TILE
    row_spec = pl.BlockSpec((CHUNK, VB), lambda i, seg: (i, 0))
    return pl.pallas_call(
        grid_kernel,
        out_shape=jax.ShapeDtypeStruct((facets, side, 2 * side), jnp.float32),
        grid_spec=pltpu.PrefetchScalarGridSpec(
            num_scalar_prefetch=1,
            grid=(blocks // CHUNK,),
            in_specs=[row_spec] * 4,
            out_specs=pl.BlockSpec((facets, side, 2 * side), lambda i, seg: (0, 0, 0)),
        ),
        cost_estimate=pl.CostEstimate(
            flops=blocks * TILE * VB * 2 * side * 2,
            bytes_accessed=blocks * VB * 16 + facets * side * 2 * side * 4,
            transcendentals=0,
        ),
    )(seg_ids, du, dv, re, im)


def dft_tables(side):
    index_ids = jnp.arange(side, dtype=jnp.int32)
    phases = index_ids[:, None] * index_ids[None, :] % side
    angles = phases.astype(jnp.float32) * (2.0 * math.pi / side)
    return (jnp.cos(angles), jnp.sin(angles))


def taps_transform(taps_row, side):
    index_ids = jnp.arange(side, dtype=jnp.int32)
    tap_ids = jnp.arange(KT, dtype=jnp.int32)
    phases = index_ids[:, None] * tap_ids[None, :] % side
    angles = phases.astype(jnp.float32) * (2.0 * math.pi / side)
    taps = taps_row.astype(jnp.float32)
    return (jnp.sum(jnp.cos(angles) * taps, axis=1), -jnp.sum(jnp.sin(angles) * taps, axis=1))


def body(voltages, block_facet, block_tile, vis_offset, kernel_taps):
    facets = lax.axis_size("stn")
    chan_count = lax.axis_size("chan")
    high = lax.Precision.HIGHEST
    panels = lax.all_to_all(voltages, "stn", split_axis=1, concat_axis=0, tiled=True)
    stations = panels.shape[0]
    local_channels = panels.shape[1]
    samples = panels.shape[2] // 2
    swapped = jnp.concatenate([panels[:, :, samples:], -panels[:, :, :samples]], axis=2)
    stacked = jnp.concatenate([panels, swapped], axis=0)
    products = jnp.einsum("aks,jks->kaj", stacked, panels, preferred_element_type=jnp.float32)
    station_ids = jnp.arange(stations, dtype=jnp.int32)
    off_diagonal = (station_ids[:, None] != station_ids[None, :]).astype(jnp.float32)
    scale = 1.0 / math.sqrt(samples)
    real_vis = (products[:, :stations, :] * scale * off_diagonal).astype(jnp.bfloat16)
    imag_vis = (products[:, stations:, :] * scale * off_diagonal).astype(jnp.bfloat16)
    re = real_vis.reshape(-1, VB).astype(jnp.float32)
    im = imag_vis.reshape(-1, VB).astype(jnp.float32)
    block_count = re.shape[0]
    offsets = vis_offset.reshape(block_count, VB)
    du = offsets // OFFS
    dv = offsets % OFFS
    seg_ids = block_facet.reshape(block_count) * TT + block_tile.reshape(block_count)
    delta = grid_blocks(seg_ids, du, dv, re, im, facets)
    side = TS * TILE
    row_count = side // chan_count
    cosine, sine = dft_tables(side)
    along_x = jnp.stack(
        [jnp.stack([cosine, sine], axis=2), jnp.stack([-sine, cosine], axis=2)], axis=1
    ).reshape(2 * side, 2 * side)
    used = jnp.arange(TS * OFFS, dtype=jnp.int32)
    used = (used // OFFS) * TILE + used % OFFS
    width = TS * OFFS
    delta = delta.reshape(facets, 2 * side, TS, TILE)[..., :OFFS].reshape(facets, 2 * side, width)
    rows = jnp.einsum("kc,fcv->kfv", along_x, delta, precision=high)
    rows = rows.reshape(chan_count * row_count * 2 * facets * width // VB, VB)
    rows = lax.all_to_all(rows, "chan", split_axis=0, concat_axis=0, tiled=True)
    rows = jnp.sum(rows.reshape(chan_count, row_count * 2, facets, width), axis=0)
    rows = jnp.transpose(rows, (1, 0, 2)).reshape(facets, row_count * 2 * width)
    rows = lax.all_to_all(rows, "stn", split_axis=0, concat_axis=0, tiled=True)
    mine = jnp.sum(rows.reshape(facets, row_count, 2, width), axis=0)
    cos_used = cosine[used]
    sin_used = sine[used]
    along_y = jnp.stack(
        [jnp.stack([cos_used, -sin_used], axis=1), jnp.stack([sin_used, cos_used], axis=1)], axis=0
    )
    spectrum = jnp.einsum("rqv,qvsy->rsy", mine, along_y, precision=high)
    first_row = lax.axis_index("chan") * row_count
    u_re, u_im = taps_transform(kernel_taps[0], side)
    v_re, v_im = taps_transform(kernel_taps[1], side)
    u_re = lax.dynamic_slice_in_dim(u_re, first_row, row_count, 0)[:, None]
    u_im = lax.dynamic_slice_in_dim(u_im, first_row, row_count, 0)[:, None]
    k_re = u_re * v_re[None, :] - u_im * v_im[None, :]
    k_im = u_re * v_im[None, :] + u_im * v_re[None, :]
    s_re = spectrum[:, 0, :]
    s_im = spectrum[:, 1, :]
    channels_all = local_channels * facets * chan_count
    norm_factor = 1.0 / math.sqrt(channels_all * stations * stations * KT * KT / facets)
    image_re = (s_re * k_re - s_im * k_im) * norm_factor
    image_im = (s_re * k_im + s_im * k_re) * norm_factor
    return jnp.stack([image_re, image_im], axis=0)


def solution(mesh):
    placed = (
        P("stn", "chan", None),
        P("chan", "stn", None, None),
        P("chan", "stn", None),
        P("chan", "stn", None, None),
        P(),
    )
    return jax.shard_map(
        body, mesh=mesh, in_specs=placed, out_specs=P(None, ("stn", "chan"), None), check_vma=False
    )
```

```python
import functools
import math

import jax
import jax.numpy as jnp
from jax import lax
from jax.experimental import pallas as pl
from jax.experimental.pallas import tpu as pltpu
from jax.sharding import PartitionSpec as P

VB = 128
TILE = 32
KT = 8
TS = 4
TT = 16
OFFS = 25
GROUP = 8


def grid_kernel(order_ref, seg_ref, bounds_ref, du_ref, dv_ref, re_ref, im_ref, out_ref):
    side = TS * TILE
    half = out_ref.shape[0]
    low = bounds_ref[2]
    out_ref[...] = jnp.zeros_like(out_ref)
    cells = lax.broadcasted_iota(jnp.int32, (TILE, VB), 0)
    lines = lax.broadcasted_iota(jnp.int32, (side, VB), 0)
    first = bounds_ref[0]
    last = bounds_ref[1]

    def one_block(j):
        valid = (j >= first) & (j < last)
        place = jnp.minimum(j, du_ref.shape[0] - 1)
        b = order_ref[place]
        du = du_ref[pl.ds(b, 1), :]
        dv = dv_ref[pl.ds(b, 1), :]
        re = jnp.where(valid, re_ref[pl.ds(b, 1), :], 0.0)
        im = jnp.where(valid, im_ref[pl.ds(b, 1), :], 0.0)
        seg = seg_ref[b]
        facet = jnp.clip(seg // TT - low, 0, half - 1)
        tile = seg % TT
        first_u = pl.multiple_of((tile // TS) * TILE, TILE)
        first_v = (tile % TS) * TILE
        along_u = (cells == du).astype(jnp.float32).astype(jnp.bfloat16)
        hit_v = lines == (dv + first_v)
        spread = jnp.concatenate(
            [jnp.where(hit_v, re, 0.0), jnp.where(hit_v, im, 0.0)], axis=0
        ).astype(jnp.bfloat16)
        tile_sum = lax.dot_general(
            along_u, spread, (((1,), (1,)), ((), ())), preferred_element_type=jnp.float32
        )
        out_ref[facet, pl.ds(first_u, TILE), :] += tile_sum

    def group(g, carry):
        for i in range(GROUP):
            one_block(g * GROUP + i)
        return carry

    lax.fori_loop(first // GROUP, (last + GROUP - 1) // GROUP, group, 0)


def grid_blocks(order, seg_ids, bounds, du, dv, re, im, half):
    blocks = du.shape[0]
    side = TS * TILE
    row_spec = pl.BlockSpec((blocks, VB), lambda i, *_: (0, 0))
    return pl.pallas_call(
        grid_kernel,
        out_shape=jax.ShapeDtypeStruct((half, side, 2 * side), jnp.float32),
        grid_spec=pltpu.PrefetchScalarGridSpec(
            num_scalar_prefetch=3,
            grid=(1,),
            in_specs=[row_spec] * 4,
            out_specs=pl.BlockSpec((half, side, 2 * side), lambda i, *_: (0, 0, 0)),
        ),
        cost_estimate=pl.CostEstimate(
            flops=blocks * TILE * VB * 2 * side,
            bytes_accessed=blocks * VB * 16 + half * side * 2 * side * 4,
            transcendentals=0,
        ),
    )(order, seg_ids, bounds, du, dv, re, im)


def dft_tables(side):
    index_ids = jnp.arange(side, dtype=jnp.int32)
    phases = index_ids[:, None] * index_ids[None, :] % side
    angles = phases.astype(jnp.float32) * (2.0 * math.pi / side)
    return (jnp.cos(angles), jnp.sin(angles))


def taps_transform(taps_row, side):
    index_ids = jnp.arange(side, dtype=jnp.int32)
    tap_ids = jnp.arange(KT, dtype=jnp.int32)
    phases = index_ids[:, None] * tap_ids[None, :] % side
    angles = phases.astype(jnp.float32) * (2.0 * math.pi / side)
    taps = taps_row.astype(jnp.float32)
    return (jnp.sum(jnp.cos(angles) * taps, axis=1), -jnp.sum(jnp.sin(angles) * taps, axis=1))


def body(voltages, block_facet, block_tile, vis_offset, kernel_taps):
    facets = lax.axis_size("stn")
    chan_count = lax.axis_size("chan")
    high = lax.Precision.HIGHEST
    panels = lax.all_to_all(voltages, "stn", split_axis=1, concat_axis=0, tiled=True)
    stations = panels.shape[0]
    local_channels = panels.shape[1]
    samples = panels.shape[2] // 2
    swapped = jnp.concatenate([panels[:, :, samples:], -panels[:, :, :samples]], axis=2)
    stacked = jnp.concatenate([panels, swapped], axis=0)
    products = jnp.einsum("aks,jks->kaj", stacked, panels, preferred_element_type=jnp.float32)
    station_ids = jnp.arange(stations, dtype=jnp.int32)
    off_diagonal = (station_ids[:, None] != station_ids[None, :]).astype(jnp.float32)
    scale = 1.0 / math.sqrt(samples)
    real_vis = (products[:, :stations, :] * scale * off_diagonal).astype(jnp.bfloat16)
    imag_vis = (products[:, stations:, :] * scale * off_diagonal).astype(jnp.bfloat16)
    re = real_vis.reshape(-1, VB).astype(jnp.float32)
    im = imag_vis.reshape(-1, VB).astype(jnp.float32)
    block_count = re.shape[0]
    offsets = vis_offset.reshape(block_count, VB)
    du = offsets // OFFS
    dv = offsets % OFFS
    seg_ids = block_facet.reshape(block_count) * TT + block_tile.reshape(block_count)
    half = facets // 2
    later = (block_facet.reshape(block_count) >= half).astype(jnp.int32)
    order = jnp.argsort(later, stable=True).astype(jnp.int32)
    split = block_count - jnp.sum(later)
    side = TS * TILE
    row_count = side // chan_count
    cosine, sine = dft_tables(side)
    along_x = jnp.stack(
        [jnp.stack([cosine, sine], axis=2), jnp.stack([-sine, cosine], axis=2)], axis=1
    ).reshape(2 * side, 2 * side)
    summed = []
    for low, first, last in ((0, 0, split), (half, split, block_count)):
        bounds = jnp.stack([first, last, low]).astype(jnp.int32)
        delta = grid_blocks(order, seg_ids, bounds, du, dv, re, im, half)
        rows = jnp.einsum("kc,fcv->kfv", along_x, delta.reshape(half, 2 * side, side), precision=high)
        rows = rows.reshape(chan_count * row_count * 2 * half, side)
        rows = lax.all_to_all(rows, "chan", split_axis=0, concat_axis=0, tiled=True)
        summed.append(jnp.sum(rows.reshape(chan_count, row_count * 2, half, side), axis=0))
    rows = jnp.concatenate(summed, axis=1)
    rows = jnp.transpose(rows, (1, 0, 2)).reshape(facets * row_count * 2, side)
    rows = lax.all_to_all(rows, "stn", split_axis=0, concat_axis=0, tiled=True)
    mine = jnp.sum(rows.reshape(facets, row_count, 2, side), axis=0)
    along_y = jnp.stack(
        [jnp.stack([cosine, -sine], axis=1), jnp.stack([sine, cosine], axis=1)], axis=0
    )
    spectrum = jnp.einsum("rqv,qvsy->rsy", mine, along_y, precision=high)
    first_row = lax.axis_index("chan") * row_count
    u_re, u_im = taps_transform(kernel_taps[0], side)
    v_re, v_im = taps_transform(kernel_taps[1], side)
    u_re = lax.dynamic_slice_in_dim(u_re, first_row, row_count, 0)[:, None]
    u_im = lax.dynamic_slice_in_dim(u_im, first_row, row_count, 0)[:, None]
    k_re = u_re * v_re[None, :] - u_im * v_im[None, :]
    k_im = u_re * v_im[None, :] + u_im * v_re[None, :]
    s_re = spectrum[:, 0, :]
    s_im = spectrum[:, 1, :]
    channels_all = local_channels * facets * chan_count
    norm_factor = 1.0 / math.sqrt(channels_all * stations * stations * KT * KT / facets)
    image_re = (s_re * k_re - s_im * k_im) * norm_factor
    image_im = (s_re * k_im + s_im * k_re) * norm_factor
    return jnp.stack([image_re, image_im], axis=0)


def solution(mesh):
    placed = (
        P("stn", "chan", None),
        P("chan", "stn", None, None),
        P("chan", "stn", None),
        P("chan", "stn", None, None),
        P(),
    )
    return jax.shard_map(
        body, mesh=mesh, in_specs=placed, out_specs=P(None, ("stn", "chan"), None), check_vma=False
    )
```

```python
import functools
import math

import jax
import jax.numpy as jnp
from jax import lax
from jax.experimental import pallas as pl
from jax.experimental.pallas import tpu as pltpu
from jax.sharding import PartitionSpec as P

VB = 128
TILE = 32
KT = 8
TS = 4
TT = 16
OFFS = 25
CHUNK = 256


def grid_kernel(seg_ref, du_ref, dv_ref, re_ref, im_ref, out_ref):
    step = pl.program_id(0)
    side = TS * TILE

    @pl.when(step == 0)
    def _():
        out_ref[...] = jnp.zeros_like(out_ref)
    cells = lax.broadcasted_iota(jnp.int32, (TILE, VB), 0)
    lines = lax.broadcasted_iota(jnp.int32, (side, VB), 0)
    def one_block(b, carry):
        du = du_ref[pl.ds(b, 1), :]
        dv = dv_ref[pl.ds(b, 1), :]
        re = re_ref[pl.ds(b, 1), :]
        im = im_ref[pl.ds(b, 1), :]
        seg = seg_ref[step * CHUNK + b]
        facet = seg // TT
        tile = seg % TT
        first_u = pl.multiple_of((tile // TS) * TILE, TILE)
        first_v = (tile % TS) * TILE
        along_u = (cells == du).astype(jnp.float32).astype(jnp.bfloat16)
        hit_v = lines == (dv + first_v)
        spread = jnp.concatenate(
            [jnp.where(hit_v, re, 0.0), jnp.where(hit_v, im, 0.0)], axis=0
        ).astype(jnp.bfloat16)
        tile_sum = lax.dot_general(
            along_u, spread, (((1,), (1,)), ((), ())), preferred_element_type=jnp.float32
        )
        out_ref[facet, pl.ds(first_u, TILE), :] += tile_sum
        return carry
    lax.fori_loop(0, CHUNK, one_block, 0, unroll=8)


def grid_blocks(seg_ids, du, dv, re, im, facets):
    blocks = du.shape[0]
    side = TS * TILE
    row_spec = pl.BlockSpec((CHUNK, VB), lambda i, seg: (i, 0))
    return pl.pallas_call(
        grid_kernel,
        out_shape=jax.ShapeDtypeStruct((facets, side, 2 * side), jnp.float32),
        grid_spec=pltpu.PrefetchScalarGridSpec(
            num_scalar_prefetch=1,
            grid=(blocks // CHUNK,),
            in_specs=[row_spec] * 4,
            out_specs=pl.BlockSpec((facets, side, 2 * side), lambda i, seg: (0, 0, 0)),
        ),
        cost_estimate=pl.CostEstimate(
            flops=blocks * TILE * VB * 2 * side * 2,
            bytes_accessed=blocks * VB * 16 + facets * side * 2 * side * 4,
            transcendentals=0,
        ),
    )(seg_ids, du, dv, re, im)


def dft_tables(side):
    index_ids = jnp.arange(side, dtype=jnp.int32)
    phases = index_ids[:, None] * index_ids[None, :] % side
    angles = phases.astype(jnp.float32) * (2.0 * math.pi / side)
    return (jnp.cos(angles), jnp.sin(angles))


def taps_transform(taps_row, side):
    index_ids = jnp.arange(side, dtype=jnp.int32)
    tap_ids = jnp.arange(KT, dtype=jnp.int32)
    phases = index_ids[:, None] * tap_ids[None, :] % side
    angles = phases.astype(jnp.float32) * (2.0 * math.pi / side)
    taps = taps_row.astype(jnp.float32)
    return (jnp.sum(jnp.cos(angles) * taps, axis=1), -jnp.sum(jnp.sin(angles) * taps, axis=1))


def body(voltages, block_facet, block_tile, vis_offset, kernel_taps):
    facets = lax.axis_size("stn")
    chan_count = lax.axis_size("chan")
    high = lax.Precision.HIGHEST
    panels = lax.all_to_all(voltages, "stn", split_axis=1, concat_axis=0, tiled=True)
    stations = panels.shape[0]
    local_channels = panels.shape[1]
    samples = panels.shape[2] // 2
    swapped = jnp.concatenate([panels[:, :, samples:], -panels[:, :, :samples]], axis=2)
    stacked = jnp.concatenate([panels, swapped], axis=0)
    products = jnp.einsum("aks,jks->kaj", stacked, panels, preferred_element_type=jnp.float32)
    station_ids = jnp.arange(stations, dtype=jnp.int32)
    off_diagonal = (station_ids[:, None] != station_ids[None, :]).astype(jnp.float32)
    scale = 1.0 / math.sqrt(samples)
    real_vis = (products[:, :stations, :] * scale * off_diagonal).astype(jnp.bfloat16)
    imag_vis = (products[:, stations:, :] * scale * off_diagonal).astype(jnp.bfloat16)
    re = real_vis.reshape(-1, VB).astype(jnp.float32)
    im = imag_vis.reshape(-1, VB).astype(jnp.float32)
    block_count = re.shape[0]
    offsets = vis_offset.reshape(block_count, VB)
    du = offsets // OFFS
    dv = offsets % OFFS
    seg_ids = block_facet.reshape(block_count) * TT + block_tile.reshape(block_count)
    delta = grid_blocks(seg_ids, du, dv, re, im, facets)
    side = TS * TILE
    row_count = side // chan_count
    cosine, sine = dft_tables(side)
    along_x = jnp.stack(
        [jnp.stack([cosine, sine], axis=2), jnp.stack([-sine, cosine], axis=2)], axis=1
    ).reshape(2 * side, 2 * side)
    rows = jnp.einsum("kc,fcv->kfv", along_x, delta.reshape(facets, 2 * side, side), precision=high)
    rows = rows.reshape(chan_count, row_count * 2, facets, side)
    rows = jnp.transpose(rows, (2, 0, 1, 3)).reshape(facets * chan_count * row_count * 2, side)
    rows = lax.all_to_all(rows, ("stn", "chan"), split_axis=0, concat_axis=0, tiled=True)
    mine = jnp.sum(rows.reshape(facets * chan_count, row_count, 2, side), axis=0)
    along_y = jnp.stack(
        [jnp.stack([cosine, -sine], axis=1), jnp.stack([sine, cosine], axis=1)], axis=0
    )
    spectrum = jnp.einsum("rqv,qvsy->rsy", mine, along_y, precision=high)
    first_row = lax.axis_index("chan") * row_count
    u_re, u_im = taps_transform(kernel_taps[0], side)
    v_re, v_im = taps_transform(kernel_taps[1], side)
    u_re = lax.dynamic_slice_in_dim(u_re, first_row, row_count, 0)[:, None]
    u_im = lax.dynamic_slice_in_dim(u_im, first_row, row_count, 0)[:, None]
    k_re = u_re * v_re[None, :] - u_im * v_im[None, :]
    k_im = u_re * v_im[None, :] + u_im * v_re[None, :]
    s_re = spectrum[:, 0, :]
    s_im = spectrum[:, 1, :]
    channels_all = local_channels * facets * chan_count
    norm_factor = 1.0 / math.sqrt(channels_all * stations * stations * KT * KT / facets)
    image_re = (s_re * k_re - s_im * k_im) * norm_factor
    image_im = (s_re * k_im + s_im * k_re) * norm_factor
    return jnp.stack([image_re, image_im], axis=0)


def solution(mesh):
    placed = (
        P("stn", "chan", None),
        P("chan", "stn", None, None),
        P("chan", "stn", None),
        P("chan", "stn", None, None),
        P(),
    )
    return jax.shard_map(
        body, mesh=mesh, in_specs=placed, out_specs=P(None, ("stn", "chan"), None), check_vma=False
    )
```

```python
import functools
import math

import jax
import jax.numpy as jnp
from jax import lax
from jax.experimental import pallas as pl
from jax.experimental.pallas import tpu as pltpu
from jax.sharding import PartitionSpec as P

VB = 128
TILE = 32
KT = 8
TS = 4
TT = 16
OFFS = 25
CHUNK = 256
SPARE = 3


def grid_kernel(seg_ref, du_ref, dv_ref, re_ref, im_ref, out_ref, spare_ref):
    step = pl.program_id(0)
    side = TS * TILE
    sums = [out_ref] + [spare_ref.at[i] for i in range(spare_ref.shape[0])]

    @pl.when(step == 0)
    def _():
        out_ref[...] = jnp.zeros_like(out_ref)
        spare_ref[...] = jnp.zeros_like(spare_ref)
    cells = lax.broadcasted_iota(jnp.int32, (TILE, VB), 0)
    lines = lax.broadcasted_iota(jnp.int32, (side, VB), 0)
    def one_block(b, total):
        du = du_ref[pl.ds(b, 1), :]
        dv = dv_ref[pl.ds(b, 1), :]
        re = re_ref[pl.ds(b, 1), :]
        im = im_ref[pl.ds(b, 1), :]
        seg = seg_ref[step * CHUNK + b]
        facet = seg // TT
        tile = seg % TT
        first_u = pl.multiple_of((tile // TS) * TILE, TILE)
        first_v = (tile % TS) * TILE
        along_u = (cells == du).astype(jnp.float32).astype(jnp.bfloat16)
        hit_v = lines == (dv + first_v)
        spread = jnp.concatenate(
            [jnp.where(hit_v, re, 0.0), jnp.where(hit_v, im, 0.0)], axis=0
        ).astype(jnp.bfloat16)
        tile_sum = lax.dot_general(
            along_u, spread, (((1,), (1,)), ((), ())), preferred_element_type=jnp.float32
        )
        total[facet, pl.ds(first_u, TILE), :] += tile_sum

    def blocks(g, carry):
        for i, total in enumerate(sums):
            one_block(g * len(sums) + i, total)
        return carry

    lax.fori_loop(0, CHUNK // len(sums), blocks, 0, unroll=2)

    @pl.when(step == pl.num_programs(0) - 1)
    def _():
        out_ref[...] += jnp.sum(spare_ref[...], axis=0)


def grid_blocks(seg_ids, du, dv, re, im, facets):
    blocks = du.shape[0]
    side = TS * TILE
    row_spec = pl.BlockSpec((CHUNK, VB), lambda i, seg: (i, 0))
    return pl.pallas_call(
        grid_kernel,
        out_shape=jax.ShapeDtypeStruct((facets, side, 2 * side), jnp.float32),
        grid_spec=pltpu.PrefetchScalarGridSpec(
            num_scalar_prefetch=1,
            grid=(blocks // CHUNK,),
            in_specs=[row_spec] * 4,
            out_specs=pl.BlockSpec((facets, side, 2 * side), lambda i, seg: (0, 0, 0)),
            scratch_shapes=[pltpu.VMEM((SPARE, facets, side, 2 * side), jnp.float32)],
        ),
        cost_estimate=pl.CostEstimate(
            flops=blocks * TILE * VB * 2 * side * 2,
            bytes_accessed=blocks * VB * 16 + facets * side * 2 * side * 4,
            transcendentals=0,
        ),
    )(seg_ids, du, dv, re, im)


def dft_tables(side):
    index_ids = jnp.arange(side, dtype=jnp.int32)
    phases = index_ids[:, None] * index_ids[None, :] % side
    angles = phases.astype(jnp.float32) * (2.0 * math.pi / side)
    return (jnp.cos(angles), jnp.sin(angles))


def taps_transform(taps_row, side):
    index_ids = jnp.arange(side, dtype=jnp.int32)
    tap_ids = jnp.arange(KT, dtype=jnp.int32)
    phases = index_ids[:, None] * tap_ids[None, :] % side
    angles = phases.astype(jnp.float32) * (2.0 * math.pi / side)
    taps = taps_row.astype(jnp.float32)
    return (jnp.sum(jnp.cos(angles) * taps, axis=1), -jnp.sum(jnp.sin(angles) * taps, axis=1))


def body(voltages, block_facet, block_tile, vis_offset, kernel_taps):
    facets = lax.axis_size("stn")
    chan_count = lax.axis_size("chan")
    high = lax.Precision.HIGHEST
    panels = lax.all_to_all(voltages, "stn", split_axis=1, concat_axis=0, tiled=True)
    stations = panels.shape[0]
    local_channels = panels.shape[1]
    samples = panels.shape[2] // 2
    swapped = jnp.concatenate([panels[:, :, samples:], -panels[:, :, :samples]], axis=2)
    stacked = jnp.concatenate([panels, swapped], axis=0)
    products = jnp.einsum("aks,jks->kaj", stacked, panels, preferred_element_type=jnp.float32)
    station_ids = jnp.arange(stations, dtype=jnp.int32)
    off_diagonal = (station_ids[:, None] != station_ids[None, :]).astype(jnp.float32)
    scale = 1.0 / math.sqrt(samples)
    real_vis = (products[:, :stations, :] * scale * off_diagonal).astype(jnp.bfloat16)
    imag_vis = (products[:, stations:, :] * scale * off_diagonal).astype(jnp.bfloat16)
    re = real_vis.reshape(-1, VB).astype(jnp.float32)
    im = imag_vis.reshape(-1, VB).astype(jnp.float32)
    block_count = re.shape[0]
    offsets = vis_offset.reshape(block_count, VB)
    du = offsets // OFFS
    dv = offsets % OFFS
    seg_ids = block_facet.reshape(block_count) * TT + block_tile.reshape(block_count)
    delta = grid_blocks(seg_ids, du, dv, re, im, facets)
    side = TS * TILE
    row_count = side // chan_count
    cosine, sine = dft_tables(side)
    along_x = jnp.stack(
        [jnp.stack([cosine, sine], axis=2), jnp.stack([-sine, cosine], axis=2)], axis=1
    ).reshape(2 * side, 2 * side)
    rows = jnp.einsum("kc,fcv->kfv", along_x, delta.reshape(facets, 2 * side, side), precision=high)
    rows = rows.reshape(chan_count, row_count * 2, facets, side)
    rows = jnp.transpose(rows, (2, 0, 1, 3)).reshape(facets * chan_count * row_count * 2, side)
    rows = lax.all_to_all(rows, ("stn", "chan"), split_axis=0, concat_axis=0, tiled=True)
    mine = jnp.sum(rows.reshape(facets * chan_count, row_count, 2, side), axis=0)
    along_y = jnp.stack(
        [jnp.stack([cosine, -sine], axis=1), jnp.stack([sine, cosine], axis=1)], axis=0
    )
    spectrum = jnp.einsum("rqv,qvsy->rsy", mine, along_y, precision=high)
    first_row = lax.axis_index("chan") * row_count
    u_re, u_im = taps_transform(kernel_taps[0], side)
    v_re, v_im = taps_transform(kernel_taps[1], side)
    u_re = lax.dynamic_slice_in_dim(u_re, first_row, row_count, 0)[:, None]
    u_im = lax.dynamic_slice_in_dim(u_im, first_row, row_count, 0)[:, None]
    k_re = u_re * v_re[None, :] - u_im * v_im[None, :]
    k_im = u_re * v_im[None, :] + u_im * v_re[None, :]
    s_re = spectrum[:, 0, :]
    s_im = spectrum[:, 1, :]
    channels_all = local_channels * facets * chan_count
    norm_factor = 1.0 / math.sqrt(channels_all * stations * stations * KT * KT / facets)
    image_re = (s_re * k_re - s_im * k_im) * norm_factor
    image_im = (s_re * k_im + s_im * k_re) * norm_factor
    return jnp.stack([image_re, image_im], axis=0)


def solution(mesh):
    placed = (
        P("stn", "chan", None),
        P("chan", "stn", None, None),
        P("chan", "stn", None),
        P("chan", "stn", None, None),
        P(),
    )
    return jax.shard_map(
        body, mesh=mesh, in_specs=placed, out_specs=P(None, ("stn", "chan"), None), check_vma=False
    )
```

```python
import functools
import math

import jax
import jax.numpy as jnp
from jax import lax
from jax.experimental import pallas as pl
from jax.experimental.pallas import tpu as pltpu
from jax.sharding import PartitionSpec as P

VB = 128
TILE = 32
KT = 8
TS = 4
TT = 16
OFFS = 25
CHUNK = 256
SPARE = 3


def grid_kernel(seg_ref, du_ref, dv_ref, re_ref, im_ref, out_ref, spare_ref):
    step = pl.program_id(0)
    side = TS * TILE
    sums = [out_ref] + [spare_ref.at[i] for i in range(spare_ref.shape[0])]

    @pl.when(step == 0)
    def _():
        out_ref[...] = jnp.zeros_like(out_ref)
        spare_ref[...] = jnp.zeros_like(spare_ref)
    cells = lax.broadcasted_iota(jnp.int32, (TILE, VB), 0)
    lines = lax.broadcasted_iota(jnp.int32, (side, VB), 0)
    def one_block(b, total):
        du = du_ref[pl.ds(b, 1), :]
        dv = dv_ref[pl.ds(b, 1), :]
        re = re_ref[pl.ds(b, 1), :]
        im = im_ref[pl.ds(b, 1), :]
        seg = seg_ref[step * CHUNK + b]
        facet = seg // TT
        tile = seg % TT
        first_u = pl.multiple_of((tile // TS) * TILE, TILE)
        first_v = (tile % TS) * TILE
        along_u = (cells == du).astype(jnp.float32).astype(jnp.bfloat16)
        hit_v = lines == (dv + first_v)
        spread = jnp.concatenate(
            [jnp.where(hit_v, re, 0.0), jnp.where(hit_v, im, 0.0)], axis=0
        ).astype(jnp.bfloat16)
        tile_sum = lax.dot_general(
            along_u, spread, (((1,), (1,)), ((), ())), preferred_element_type=jnp.float32
        )
        total[facet, pl.ds(first_u, TILE), :] += tile_sum

    def blocks(g, carry):
        for i, total in enumerate(sums):
            one_block(g * len(sums) + i, total)
        return carry

    lax.fori_loop(0, CHUNK // len(sums), blocks, 0, unroll=2)

    @pl.when(step == pl.num_programs(0) - 1)
    def _():
        out_ref[...] += jnp.sum(spare_ref[...], axis=0)


def grid_blocks(seg_ids, du, dv, re, im, facets):
    blocks = du.shape[0]
    side = TS * TILE
    row_spec = pl.BlockSpec((CHUNK, VB), lambda i, seg: (i, 0))
    return pl.pallas_call(
        grid_kernel,
        out_shape=jax.ShapeDtypeStruct((facets, side, 2 * side), jnp.float32),
        grid_spec=pltpu.PrefetchScalarGridSpec(
            num_scalar_prefetch=1,
            grid=(blocks // CHUNK,),
            in_specs=[row_spec] * 4,
            out_specs=pl.BlockSpec((facets, side, 2 * side), lambda i, seg: (0, 0, 0)),
            scratch_shapes=[pltpu.VMEM((SPARE, facets, side, 2 * side), jnp.float32)],
        ),
        cost_estimate=pl.CostEstimate(
            flops=blocks * TILE * VB * 2 * side * 2,
            bytes_accessed=blocks * VB * 16 + facets * side * 2 * side * 4,
            transcendentals=0,
        ),
    )(seg_ids, du, dv, re, im)


def dft_tables(side):
    index_ids = jnp.arange(side, dtype=jnp.int32)
    phases = index_ids[:, None] * index_ids[None, :] % side
    angles = phases.astype(jnp.float32) * (2.0 * math.pi / side)
    return (jnp.cos(angles), jnp.sin(angles))


def complex_table(side, row_major, sign):
    shape = (side, 2, side, 2) if row_major else (2, side, 2, side)
    axes = (0, 1, 2, 3) if row_major else (1, 0, 3, 2)
    first = lax.broadcasted_iota(jnp.int32, shape, axes[0])
    part_in = lax.broadcasted_iota(jnp.int32, shape, axes[1])
    second = lax.broadcasted_iota(jnp.int32, shape, axes[2])
    part_out = lax.broadcasted_iota(jnp.int32, shape, axes[3])
    angles = (first * second % side).astype(jnp.float32) * (2.0 * math.pi / side)
    cross = jnp.where(part_in == 0, sign, -sign) * jnp.sin(angles)
    return jnp.where(part_in == part_out, jnp.cos(angles), cross)


def taps_transform(taps_row, side):
    index_ids = jnp.arange(side, dtype=jnp.int32)
    tap_ids = jnp.arange(KT, dtype=jnp.int32)
    phases = index_ids[:, None] * tap_ids[None, :] % side
    angles = phases.astype(jnp.float32) * (2.0 * math.pi / side)
    taps = taps_row.astype(jnp.float32)
    return (jnp.sum(jnp.cos(angles) * taps, axis=1), -jnp.sum(jnp.sin(angles) * taps, axis=1))


def body(voltages, block_facet, block_tile, vis_offset, kernel_taps):
    facets = lax.axis_size("stn")
    chan_count = lax.axis_size("chan")
    high = lax.Precision.HIGHEST
    panels = lax.all_to_all(voltages, "stn", split_axis=1, concat_axis=0, tiled=True)
    stations = panels.shape[0]
    local_channels = panels.shape[1]
    samples = panels.shape[2] // 2
    swapped = jnp.concatenate([panels[:, :, samples:], -panels[:, :, :samples]], axis=2)
    stacked = jnp.concatenate([panels, swapped], axis=0)
    products = jnp.einsum("aks,jks->kaj", stacked, panels, preferred_element_type=jnp.float32)
    station_ids = jnp.arange(stations, dtype=jnp.int32)
    off_diagonal = (station_ids[:, None] != station_ids[None, :]).astype(jnp.float32)
    scale = 1.0 / math.sqrt(samples)
    real_vis = (products[:, :stations, :] * scale * off_diagonal).astype(jnp.bfloat16)
    imag_vis = (products[:, stations:, :] * scale * off_diagonal).astype(jnp.bfloat16)
    re = real_vis.reshape(-1, VB).astype(jnp.float32)
    im = imag_vis.reshape(-1, VB).astype(jnp.float32)
    block_count = re.shape[0]
    offsets = vis_offset.reshape(block_count, VB)
    du = offsets // OFFS
    dv = offsets % OFFS
    seg_ids = block_facet.reshape(block_count) * TT + block_tile.reshape(block_count)
    delta = grid_blocks(seg_ids, du, dv, re, im, facets)
    side = TS * TILE
    row_count = side // chan_count
    along_x = complex_table(side, True, 1.0).reshape(2 * side, 2 * side)
    rows = jnp.einsum("kc,fcv->kfv", along_x, delta.reshape(facets, 2 * side, side), precision=high)
    rows = rows.reshape(chan_count, row_count * 2, facets, side)
    rows = jnp.transpose(rows, (2, 0, 1, 3)).reshape(facets * chan_count * row_count * 2, side)
    rows = lax.all_to_all(rows, ("stn", "chan"), split_axis=0, concat_axis=0, tiled=True)
    mine = jnp.sum(rows.reshape(facets * chan_count, row_count, 2, side), axis=0)
    along_y = complex_table(side, False, -1.0)
    spectrum = jnp.einsum("rqv,qvsy->rsy", mine, along_y, precision=high)
    first_row = lax.axis_index("chan") * row_count
    u_re, u_im = taps_transform(kernel_taps[0], side)
    v_re, v_im = taps_transform(kernel_taps[1], side)
    u_re = lax.dynamic_slice_in_dim(u_re, first_row, row_count, 0)[:, None]
    u_im = lax.dynamic_slice_in_dim(u_im, first_row, row_count, 0)[:, None]
    k_re = u_re * v_re[None, :] - u_im * v_im[None, :]
    k_im = u_re * v_im[None, :] + u_im * v_re[None, :]
    s_re = spectrum[:, 0, :]
    s_im = spectrum[:, 1, :]
    channels_all = local_channels * facets * chan_count
    norm_factor = 1.0 / math.sqrt(channels_all * stations * stations * KT * KT / facets)
    image_re = (s_re * k_re - s_im * k_im) * norm_factor
    image_im = (s_re * k_im + s_im * k_re) * norm_factor
    return jnp.stack([image_re, image_im], axis=0)


def solution(mesh):
    placed = (
        P("stn", "chan", None),
        P("chan", "stn", None, None),
        P("chan", "stn", None),
        P("chan", "stn", None, None),
        P(),
    )
    return jax.shard_map(
        body, mesh=mesh, in_specs=placed, out_specs=P(None, ("stn", "chan"), None), check_vma=False
    )
```

```python
import functools
import math

import jax
import jax.numpy as jnp
from jax import lax
from jax.experimental import pallas as pl
from jax.experimental.pallas import tpu as pltpu
from jax.sharding import PartitionSpec as P

VB = 128
TILE = 32
KT = 8
TS = 4
TT = 16
OFFS = 25
CHUNK = 256


def grid_kernel(seg_ref, du_ref, dv_ref, re_ref, im_ref, out_ref):
    step = pl.program_id(0)
    side = TS * TILE

    @pl.when(step == 0)
    def _():
        out_ref[...] = jnp.zeros_like(out_ref)
    lines = lax.broadcasted_iota(jnp.int32, (side, VB), 0)
    def one_block(b, carry):
        du = du_ref[pl.ds(b, 1), :]
        dv = dv_ref[pl.ds(b, 1), :]
        re = re_ref[pl.ds(b, 1), :]
        im = im_ref[pl.ds(b, 1), :]
        seg = seg_ref[step * CHUNK + b]
        facet = seg // TT
        tile = seg % TT
        first_u = (tile // TS) * TILE
        first_v = (tile % TS) * TILE
        along_u = (lines == du + first_u).astype(jnp.float32).astype(jnp.bfloat16)
        hit_v = lines == (dv + first_v)
        spread = jnp.concatenate(
            [jnp.where(hit_v, re, 0.0), jnp.where(hit_v, im, 0.0)], axis=0
        ).astype(jnp.bfloat16)
        tile_sum = lax.dot_general(
            along_u, spread, (((1,), (1,)), ((), ())), preferred_element_type=jnp.float32
        )
        out_ref[facet] += tile_sum
        return carry
    lax.fori_loop(0, CHUNK, one_block, 0, unroll=8)


def grid_blocks(seg_ids, du, dv, re, im, facets):
    blocks = du.shape[0]
    side = TS * TILE
    row_spec = pl.BlockSpec((CHUNK, VB), lambda i, seg: (i, 0))
    return pl.pallas_call(
        grid_kernel,
        out_shape=jax.ShapeDtypeStruct((facets, side, 2 * side), jnp.float32),
        grid_spec=pltpu.PrefetchScalarGridSpec(
            num_scalar_prefetch=1,
            grid=(blocks // CHUNK,),
            in_specs=[row_spec] * 4,
            out_specs=pl.BlockSpec((facets, side, 2 * side), lambda i, seg: (0, 0, 0)),
        ),
        cost_estimate=pl.CostEstimate(
            flops=blocks * TILE * VB * 2 * side * 2,
            bytes_accessed=blocks * VB * 16 + facets * side * 2 * side * 4,
            transcendentals=0,
        ),
    )(seg_ids, du, dv, re, im)


def dft_tables(side):
    index_ids = jnp.arange(side, dtype=jnp.int32)
    phases = index_ids[:, None] * index_ids[None, :] % side
    angles = phases.astype(jnp.float32) * (2.0 * math.pi / side)
    return (jnp.cos(angles), jnp.sin(angles))


def taps_transform(taps_row, side):
    index_ids = jnp.arange(side, dtype=jnp.int32)
    tap_ids = jnp.arange(KT, dtype=jnp.int32)
    phases = index_ids[:, None] * tap_ids[None, :] % side
    angles = phases.astype(jnp.float32) * (2.0 * math.pi / side)
    taps = taps_row.astype(jnp.float32)
    return (jnp.sum(jnp.cos(angles) * taps, axis=1), -jnp.sum(jnp.sin(angles) * taps, axis=1))


def body(voltages, block_facet, block_tile, vis_offset, kernel_taps):
    facets = lax.axis_size("stn")
    chan_count = lax.axis_size("chan")
    high = lax.Precision.HIGHEST
    panels = lax.all_to_all(voltages, "stn", split_axis=1, concat_axis=0, tiled=True)
    stations = panels.shape[0]
    local_channels = panels.shape[1]
    samples = panels.shape[2] // 2
    swapped = jnp.concatenate([panels[:, :, samples:], -panels[:, :, :samples]], axis=2)
    stacked = jnp.concatenate([panels, swapped], axis=0)
    products = jnp.einsum("aks,jks->kaj", stacked, panels, preferred_element_type=jnp.float32)
    station_ids = jnp.arange(stations, dtype=jnp.int32)
    off_diagonal = (station_ids[:, None] != station_ids[None, :]).astype(jnp.float32)
    scale = 1.0 / math.sqrt(samples)
    real_vis = (products[:, :stations, :] * scale * off_diagonal).astype(jnp.bfloat16)
    imag_vis = (products[:, stations:, :] * scale * off_diagonal).astype(jnp.bfloat16)
    re = real_vis.reshape(-1, VB).astype(jnp.float32)
    im = imag_vis.reshape(-1, VB).astype(jnp.float32)
    block_count = re.shape[0]
    offsets = vis_offset.reshape(block_count, VB)
    du = offsets // OFFS
    dv = offsets % OFFS
    seg_ids = block_facet.reshape(block_count) * TT + block_tile.reshape(block_count)
    delta = grid_blocks(seg_ids, du, dv, re, im, facets)
    side = TS * TILE
    row_count = side // chan_count
    cosine, sine = dft_tables(side)
    along_x = jnp.stack(
        [jnp.stack([cosine, sine], axis=2), jnp.stack([-sine, cosine], axis=2)], axis=1
    ).reshape(2 * side, 2 * side)
    rows = jnp.einsum("kc,fcv->kfv", along_x, delta.reshape(facets, 2 * side, side), precision=high)
    rows = rows.reshape(chan_count, row_count * 2, facets, side)
    rows = jnp.transpose(rows, (2, 0, 1, 3)).reshape(facets * chan_count * row_count * 2, side)
    rows = lax.all_to_all(rows, ("stn", "chan"), split_axis=0, concat_axis=0, tiled=True)
    mine = jnp.sum(rows.reshape(facets * chan_count, row_count, 2, side), axis=0)
    along_y = jnp.stack(
        [jnp.stack([cosine, -sine], axis=1), jnp.stack([sine, cosine], axis=1)], axis=0
    )
    spectrum = jnp.einsum("rqv,qvsy->rsy", mine, along_y, precision=high)
    first_row = lax.axis_index("chan") * row_count
    u_re, u_im = taps_transform(kernel_taps[0], side)
    v_re, v_im = taps_transform(kernel_taps[1], side)
    u_re = lax.dynamic_slice_in_dim(u_re, first_row, row_count, 0)[:, None]
    u_im = lax.dynamic_slice_in_dim(u_im, first_row, row_count, 0)[:, None]
    k_re = u_re * v_re[None, :] - u_im * v_im[None, :]
    k_im = u_re * v_im[None, :] + u_im * v_re[None, :]
    s_re = spectrum[:, 0, :]
    s_im = spectrum[:, 1, :]
    channels_all = local_channels * facets * chan_count
    norm_factor = 1.0 / math.sqrt(channels_all * stations * stations * KT * KT / facets)
    image_re = (s_re * k_re - s_im * k_im) * norm_factor
    image_im = (s_re * k_im + s_im * k_re) * norm_factor
    return jnp.stack([image_re, image_im], axis=0)


def solution(mesh):
    placed = (
        P("stn", "chan", None),
        P("chan", "stn", None, None),
        P("chan", "stn", None),
        P("chan", "stn", None, None),
        P(),
    )
    return jax.shard_map(
        body, mesh=mesh, in_specs=placed, out_specs=P(None, ("stn", "chan"), None), check_vma=False
    )
```

```python
import functools
import math

import jax
import jax.numpy as jnp
from jax import lax
from jax.experimental import pallas as pl
from jax.experimental.pallas import tpu as pltpu
from jax.sharding import PartitionSpec as P

VB = 128
TILE = 32
KT = 8
TS = 4
TT = 16
OFFS = 25
CHUNK = 256


def grid_kernel(seg_ref, du_ref, dv_ref, re_ref, im_ref, out_ref, acc_ref):
    step = pl.program_id(0)
    side = TS * TILE

    @pl.when(step == 0)
    def _():
        acc_ref[...] = jnp.zeros_like(acc_ref)

    cells = lax.broadcasted_iota(jnp.int32, (TILE, VB), 0)

    def one_block(b, carry):
        du = du_ref[pl.ds(b, 1), :]
        dv = dv_ref[pl.ds(b, 1), :]
        re = re_ref[pl.ds(b, 1), :]
        im = im_ref[pl.ds(b, 1), :]
        seg = seg_ref[step * CHUNK + b]
        facet = seg // TT
        tile = seg % TT
        first_u = pl.multiple_of((tile // TS) * TILE, TILE)
        along_u = (cells == du).astype(jnp.float32).astype(jnp.bfloat16)
        hit_v = cells == dv
        spread = jnp.concatenate(
            [jnp.where(hit_v, re, 0.0), jnp.where(hit_v, im, 0.0)], axis=0
        ).astype(jnp.bfloat16)
        tile_sum = lax.dot_general(
            along_u, spread, (((1,), (1,)), ((), ())), preferred_element_type=jnp.float32
        )
        acc_ref[facet, tile % TS, pl.ds(first_u, TILE), :] += tile_sum
        return carry

    lax.fori_loop(0, CHUNK, one_block, 0, unroll=8)

    @pl.when(step == pl.num_programs(0) - 1)
    def _():
        rows = lax.broadcasted_iota(jnp.int32, (2 * TILE, 2 * side), 0)
        cols = lax.broadcasted_iota(jnp.int32, (2 * TILE, 2 * side), 1)
        places = [
            (cols == (rows // TILE) * side + tv * TILE + rows % TILE).astype(jnp.float32).astype(jnp.bfloat16)
            for tv in range(TS)
        ]

        def one_facet(f, carry):
            total = jnp.zeros((side, 2 * side), jnp.float32)
            for tv in range(TS):
                part = acc_ref[f, tv]
                high = part.astype(jnp.bfloat16)
                low = (part - high.astype(jnp.float32)).astype(jnp.bfloat16)
                total = total + jnp.dot(high, places[tv], preferred_element_type=jnp.float32)
                total = total + jnp.dot(low, places[tv], preferred_element_type=jnp.float32)
            out_ref[f] = total
            return carry

        lax.fori_loop(0, out_ref.shape[0], one_facet, 0)


def grid_blocks(seg_ids, du, dv, re, im, facets):
    blocks = du.shape[0]
    side = TS * TILE
    row_spec = pl.BlockSpec((CHUNK, VB), lambda i, seg: (i, 0))
    return pl.pallas_call(
        grid_kernel,
        out_shape=jax.ShapeDtypeStruct((facets, side, 2 * side), jnp.float32),
        grid_spec=pltpu.PrefetchScalarGridSpec(
            num_scalar_prefetch=1,
            grid=(blocks // CHUNK,),
            in_specs=[row_spec] * 4,
            out_specs=pl.BlockSpec((facets, side, 2 * side), lambda i, seg: (0, 0, 0)),
            scratch_shapes=[pltpu.VMEM((facets, TS, side, 2 * TILE), jnp.float32)],
        ),
        cost_estimate=pl.CostEstimate(
            flops=blocks * TILE * VB * 2 * TILE * 2,
            bytes_accessed=blocks * VB * 16 + facets * side * 2 * side * 4,
            transcendentals=0,
        ),
    )(seg_ids, du, dv, re, im)


def dft_tables(side):
    index_ids = jnp.arange(side, dtype=jnp.int32)
    phases = index_ids[:, None] * index_ids[None, :] % side
    angles = phases.astype(jnp.float32) * (2.0 * math.pi / side)
    return (jnp.cos(angles), jnp.sin(angles))


def taps_transform(taps_row, side):
    index_ids = jnp.arange(side, dtype=jnp.int32)
    tap_ids = jnp.arange(KT, dtype=jnp.int32)
    phases = index_ids[:, None] * tap_ids[None, :] % side
    angles = phases.astype(jnp.float32) * (2.0 * math.pi / side)
    taps = taps_row.astype(jnp.float32)
    return (jnp.sum(jnp.cos(angles) * taps, axis=1), -jnp.sum(jnp.sin(angles) * taps, axis=1))


def body(voltages, block_facet, block_tile, vis_offset, kernel_taps):
    facets = lax.axis_size("stn")
    chan_count = lax.axis_size("chan")
    high = lax.Precision.HIGHEST
    panels = lax.all_to_all(voltages, "stn", split_axis=1, concat_axis=0, tiled=True)
    stations = panels.shape[0]
    local_channels = panels.shape[1]
    samples = panels.shape[2] // 2
    swapped = jnp.concatenate([panels[:, :, samples:], -panels[:, :, :samples]], axis=2)
    stacked = jnp.concatenate([panels, swapped], axis=0)
    products = jnp.einsum("aks,jks->kaj", stacked, panels, preferred_element_type=jnp.float32)
    station_ids = jnp.arange(stations, dtype=jnp.int32)
    off_diagonal = (station_ids[:, None] != station_ids[None, :]).astype(jnp.float32)
    scale = 1.0 / math.sqrt(samples)
    real_vis = (products[:, :stations, :] * scale * off_diagonal).astype(jnp.bfloat16)
    imag_vis = (products[:, stations:, :] * scale * off_diagonal).astype(jnp.bfloat16)
    re = real_vis.reshape(-1, VB).astype(jnp.float32)
    im = imag_vis.reshape(-1, VB).astype(jnp.float32)
    block_count = re.shape[0]
    offsets = vis_offset.reshape(block_count, VB)
    du = offsets // OFFS
    dv = offsets % OFFS
    seg_ids = block_facet.reshape(block_count) * TT + block_tile.reshape(block_count)
    delta = grid_blocks(seg_ids, du, dv, re, im, facets)
    side = TS * TILE
    row_count = side // chan_count
    cosine, sine = dft_tables(side)
    along_x = jnp.stack(
        [jnp.stack([cosine, sine], axis=2), jnp.stack([-sine, cosine], axis=2)], axis=1
    ).reshape(2 * side, 2 * side)
    rows = jnp.einsum("kc,fcv->kfv", along_x, delta.reshape(facets, 2 * side, side), precision=high)
    rows = rows.reshape(chan_count, row_count * 2, facets, side)
    rows = jnp.transpose(rows, (2, 0, 1, 3)).reshape(facets * chan_count * row_count * 2, side)
    rows = lax.all_to_all(rows, ("stn", "chan"), split_axis=0, concat_axis=0, tiled=True)
    mine = jnp.sum(rows.reshape(facets * chan_count, row_count, 2, side), axis=0)
    along_y = jnp.stack(
        [jnp.stack([cosine, -sine], axis=1), jnp.stack([sine, cosine], axis=1)], axis=0
    )
    spectrum = jnp.einsum("rqv,qvsy->rsy", mine, along_y, precision=high)
    first_row = lax.axis_index("chan") * row_count
    u_re, u_im = taps_transform(kernel_taps[0], side)
    v_re, v_im = taps_transform(kernel_taps[1], side)
    u_re = lax.dynamic_slice_in_dim(u_re, first_row, row_count, 0)[:, None]
    u_im = lax.dynamic_slice_in_dim(u_im, first_row, row_count, 0)[:, None]
    k_re = u_re * v_re[None, :] - u_im * v_im[None, :]
    k_im = u_re * v_im[None, :] + u_im * v_re[None, :]
    s_re = spectrum[:, 0, :]
    s_im = spectrum[:, 1, :]
    channels_all = local_channels * facets * chan_count
    norm_factor = 1.0 / math.sqrt(channels_all * stations * stations * KT * KT / facets)
    image_re = (s_re * k_re - s_im * k_im) * norm_factor
    image_im = (s_re * k_im + s_im * k_re) * norm_factor
    return jnp.stack([image_re, image_im], axis=0)


def solution(mesh):
    placed = (
        P("stn", "chan", None),
        P("chan", "stn", None, None),
        P("chan", "stn", None),
        P("chan", "stn", None, None),
        P(),
    )
    return jax.shard_map(
        body, mesh=mesh, in_specs=placed, out_specs=P(None, ("stn", "chan"), None), check_vma=False
    )
```

```python
import functools
import math

import jax
import jax.numpy as jnp
from jax import lax
from jax.experimental import pallas as pl
from jax.experimental.pallas import tpu as pltpu
from jax.sharding import PartitionSpec as P

VB = 128
TILE = 32
KT = 8
TS = 4
TT = 16
OFFS = 25
CHUNK = 512


def grid_kernel(seg_ref, du_ref, dv_ref, re_ref, im_ref, out_ref, acc_ref):
    step = pl.program_id(0)
    side = TS * TILE

    @pl.when(step == 0)
    def _():
        acc_ref[...] = jnp.zeros_like(acc_ref)

    cells = lax.broadcasted_iota(jnp.int32, (TILE, VB), 0)

    def one_block(b, carry):
        du = du_ref[pl.ds(b, 1), :]
        dv = dv_ref[pl.ds(b, 1), :]
        re = re_ref[pl.ds(b, 1), :]
        im = im_ref[pl.ds(b, 1), :]
        seg = seg_ref[step * CHUNK + b]
        facet = seg // TT
        tile = seg % TT
        first_u = pl.multiple_of((tile // TS) * TILE, TILE)
        along_u = (cells == du).astype(jnp.float32).astype(jnp.bfloat16)
        hit_v = cells == dv
        spread = jnp.concatenate(
            [jnp.where(hit_v, re, 0.0), jnp.where(hit_v, im, 0.0)], axis=0
        ).astype(jnp.bfloat16)
        tile_sum = lax.dot_general(
            along_u, spread, (((1,), (1,)), ((), ())), preferred_element_type=jnp.float32
        )
        acc_ref[facet, tile % TS, pl.ds(first_u, TILE), :] += tile_sum
        return carry

    lax.fori_loop(0, CHUNK, one_block, 0, unroll=16)

    @pl.when(step == pl.num_programs(0) - 1)
    def _():
        rows = lax.broadcasted_iota(jnp.int32, (2 * TILE, 2 * side), 0)
        cols = lax.broadcasted_iota(jnp.int32, (2 * TILE, 2 * side), 1)
        places = [
            (cols == (rows // TILE) * side + tv * TILE + rows % TILE).astype(jnp.float32).astype(jnp.bfloat16)
            for tv in range(TS)
        ]

        def one_facet(f, carry):
            total = jnp.zeros((side, 2 * side), jnp.float32)
            for tv in range(TS):
                part = acc_ref[f, tv]
                high = part.astype(jnp.bfloat16)
                low = (part - high.astype(jnp.float32)).astype(jnp.bfloat16)
                total = total + jnp.dot(high, places[tv], preferred_element_type=jnp.float32)
                total = total + jnp.dot(low, places[tv], preferred_element_type=jnp.float32)
            out_ref[f] = total
            return carry

        lax.fori_loop(0, out_ref.shape[0], one_facet, 0)


def grid_blocks(seg_ids, du, dv, re, im, facets):
    blocks = du.shape[0]
    side = TS * TILE
    row_spec = pl.BlockSpec((CHUNK, VB), lambda i, seg: (i, 0))
    return pl.pallas_call(
        grid_kernel,
        out_shape=jax.ShapeDtypeStruct((facets, side, 2 * side), jnp.float32),
        grid_spec=pltpu.PrefetchScalarGridSpec(
            num_scalar_prefetch=1,
            grid=(blocks // CHUNK,),
            in_specs=[row_spec] * 4,
            out_specs=pl.BlockSpec((facets, side, 2 * side), lambda i, seg: (0, 0, 0)),
            scratch_shapes=[pltpu.VMEM((facets, TS, side, 2 * TILE), jnp.float32)],
        ),
        cost_estimate=pl.CostEstimate(
            flops=blocks * TILE * VB * 2 * TILE * 2,
            bytes_accessed=blocks * VB * 16 + facets * side * 2 * side * 4,
            transcendentals=0,
        ),
    )(seg_ids, du, dv, re, im)


def dft_tables(side):
    index_ids = jnp.arange(side, dtype=jnp.int32)
    phases = index_ids[:, None] * index_ids[None, :] % side
    angles = phases.astype(jnp.float32) * (2.0 * math.pi / side)
    return (jnp.cos(angles), jnp.sin(angles))


def taps_transform(taps_row, side):
    index_ids = jnp.arange(side, dtype=jnp.int32)
    tap_ids = jnp.arange(KT, dtype=jnp.int32)
    phases = index_ids[:, None] * tap_ids[None, :] % side
    angles = phases.astype(jnp.float32) * (2.0 * math.pi / side)
    taps = taps_row.astype(jnp.float32)
    return (jnp.sum(jnp.cos(angles) * taps, axis=1), -jnp.sum(jnp.sin(angles) * taps, axis=1))


def body(voltages, block_facet, block_tile, vis_offset, kernel_taps):
    facets = lax.axis_size("stn")
    chan_count = lax.axis_size("chan")
    high = lax.Precision.HIGHEST
    panels = lax.all_to_all(voltages, "stn", split_axis=1, concat_axis=0, tiled=True)
    stations = panels.shape[0]
    local_channels = panels.shape[1]
    samples = panels.shape[2] // 2
    swapped = jnp.concatenate([panels[:, :, samples:], -panels[:, :, :samples]], axis=2)
    stacked = jnp.concatenate([panels, swapped], axis=0)
    products = jnp.einsum("aks,jks->kaj", stacked, panels, preferred_element_type=jnp.float32)
    station_ids = jnp.arange(stations, dtype=jnp.int32)
    off_diagonal = (station_ids[:, None] != station_ids[None, :]).astype(jnp.float32)
    scale = 1.0 / math.sqrt(samples)
    real_vis = (products[:, :stations, :] * scale * off_diagonal).astype(jnp.bfloat16)
    imag_vis = (products[:, stations:, :] * scale * off_diagonal).astype(jnp.bfloat16)
    re = real_vis.reshape(-1, VB).astype(jnp.float32)
    im = imag_vis.reshape(-1, VB).astype(jnp.float32)
    block_count = re.shape[0]
    offsets = vis_offset.reshape(block_count, VB)
    du = offsets // OFFS
    dv = offsets % OFFS
    seg_ids = block_facet.reshape(block_count) * TT + block_tile.reshape(block_count)
    delta = grid_blocks(seg_ids, du, dv, re, im, facets)
    side = TS * TILE
    row_count = side // chan_count
    cosine, sine = dft_tables(side)
    along_x = jnp.stack(
        [jnp.stack([cosine, sine], axis=2), jnp.stack([-sine, cosine], axis=2)], axis=1
    ).reshape(2 * side, 2 * side)
    rows = jnp.einsum("kc,fcv->kfv", along_x, delta.reshape(facets, 2 * side, side), precision=high)
    rows = rows.reshape(chan_count, row_count * 2, facets, side)
    rows = jnp.transpose(rows, (2, 0, 1, 3)).reshape(facets * chan_count * row_count * 2, side)
    rows = lax.all_to_all(rows, ("stn", "chan"), split_axis=0, concat_axis=0, tiled=True)
    mine = jnp.sum(rows.reshape(facets * chan_count, row_count, 2, side), axis=0)
    along_y = jnp.stack(
        [jnp.stack([cosine, -sine], axis=1), jnp.stack([sine, cosine], axis=1)], axis=0
    )
    spectrum = jnp.einsum("rqv,qvsy->rsy", mine, along_y, precision=high)
    first_row = lax.axis_index("chan") * row_count
    u_re, u_im = taps_transform(kernel_taps[0], side)
    v_re, v_im = taps_transform(kernel_taps[1], side)
    u_re = lax.dynamic_slice_in_dim(u_re, first_row, row_count, 0)[:, None]
    u_im = lax.dynamic_slice_in_dim(u_im, first_row, row_count, 0)[:, None]
    k_re = u_re * v_re[None, :] - u_im * v_im[None, :]
    k_im = u_re * v_im[None, :] + u_im * v_re[None, :]
    s_re = spectrum[:, 0, :]
    s_im = spectrum[:, 1, :]
    channels_all = local_channels * facets * chan_count
    norm_factor = 1.0 / math.sqrt(channels_all * stations * stations * KT * KT / facets)
    image_re = (s_re * k_re - s_im * k_im) * norm_factor
    image_im = (s_re * k_im + s_im * k_re) * norm_factor
    return jnp.stack([image_re, image_im], axis=0)


def solution(mesh):
    placed = (
        P("stn", "chan", None),
        P("chan", "stn", None, None),
        P("chan", "stn", None),
        P("chan", "stn", None, None),
        P(),
    )
    return jax.shard_map(
        body, mesh=mesh, in_specs=placed, out_specs=P(None, ("stn", "chan"), None), check_vma=False
    )
```

```python
import functools
import math

import jax
import jax.numpy as jnp
from jax import lax
from jax.experimental import pallas as pl
from jax.experimental.pallas import tpu as pltpu
from jax.sharding import PartitionSpec as P

VB = 128
TILE = 32
KT = 8
TS = 4
TT = 16
OFFS = 25
CHUNK = 1024


def grid_kernel(seg_ref, du_ref, dv_ref, re_ref, im_ref, out_ref, acc_ref):
    step = pl.program_id(0)
    side = TS * TILE

    @pl.when(step == 0)
    def _():
        acc_ref[...] = jnp.zeros_like(acc_ref)

    cells = lax.broadcasted_iota(jnp.int32, (TILE, VB), 0)

    def one_block(b, carry):
        du = du_ref[pl.ds(b, 1), :]
        dv = dv_ref[pl.ds(b, 1), :]
        re = re_ref[pl.ds(b, 1), :]
        im = im_ref[pl.ds(b, 1), :]
        seg = seg_ref[step * CHUNK + b]
        facet = seg // TT
        tile = seg % TT
        first_u = pl.multiple_of((tile // TS) * TILE, TILE)
        along_u = (cells == du).astype(jnp.float32).astype(jnp.bfloat16)
        hit_v = cells == dv
        spread = jnp.concatenate(
            [jnp.where(hit_v, re, 0.0), jnp.where(hit_v, im, 0.0)], axis=0
        ).astype(jnp.bfloat16)
        tile_sum = lax.dot_general(
            along_u, spread, (((1,), (1,)), ((), ())), preferred_element_type=jnp.float32
        )
        acc_ref[facet, tile % TS, pl.ds(first_u, TILE), :] += tile_sum
        return carry

    lax.fori_loop(0, CHUNK, one_block, 0, unroll=32)

    @pl.when(step == pl.num_programs(0) - 1)
    def _():
        rows = lax.broadcasted_iota(jnp.int32, (2 * TILE, 2 * side), 0)
        cols = lax.broadcasted_iota(jnp.int32, (2 * TILE, 2 * side), 1)
        places = [
            (cols == (rows // TILE) * side + tv * TILE + rows % TILE).astype(jnp.float32).astype(jnp.bfloat16)
            for tv in range(TS)
        ]

        def one_facet(f, carry):
            total = jnp.zeros((side, 2 * side), jnp.float32)
            for tv in range(TS):
                part = acc_ref[f, tv]
                high = part.astype(jnp.bfloat16)
                low = (part - high.astype(jnp.float32)).astype(jnp.bfloat16)
                total = total + jnp.dot(high, places[tv], preferred_element_type=jnp.float32)
                total = total + jnp.dot(low, places[tv], preferred_element_type=jnp.float32)
            out_ref[f] = total
            return carry

        lax.fori_loop(0, out_ref.shape[0], one_facet, 0)


def grid_blocks(seg_ids, du, dv, re, im, facets):
    blocks = du.shape[0]
    side = TS * TILE
    row_spec = pl.BlockSpec((CHUNK, VB), lambda i, seg: (i, 0))
    return pl.pallas_call(
        grid_kernel,
        out_shape=jax.ShapeDtypeStruct((facets, side, 2 * side), jnp.float32),
        grid_spec=pltpu.PrefetchScalarGridSpec(
            num_scalar_prefetch=1,
            grid=(blocks // CHUNK,),
            in_specs=[row_spec] * 4,
            out_specs=pl.BlockSpec((facets, side, 2 * side), lambda i, seg: (0, 0, 0)),
            scratch_shapes=[pltpu.VMEM((facets, TS, side, 2 * TILE), jnp.float32)],
        ),
        cost_estimate=pl.CostEstimate(
            flops=blocks * TILE * VB * 2 * TILE * 2,
            bytes_accessed=blocks * VB * 16 + facets * side * 2 * side * 4,
            transcendentals=0,
        ),
    )(seg_ids, du, dv, re, im)


def dft_tables(side):
    index_ids = jnp.arange(side, dtype=jnp.int32)
    phases = index_ids[:, None] * index_ids[None, :] % side
    angles = phases.astype(jnp.float32) * (2.0 * math.pi / side)
    return (jnp.cos(angles), jnp.sin(angles))


def taps_transform(taps_row, side):
    index_ids = jnp.arange(side, dtype=jnp.int32)
    tap_ids = jnp.arange(KT, dtype=jnp.int32)
    phases = index_ids[:, None] * tap_ids[None, :] % side
    angles = phases.astype(jnp.float32) * (2.0 * math.pi / side)
    taps = taps_row.astype(jnp.float32)
    return (jnp.sum(jnp.cos(angles) * taps, axis=1), -jnp.sum(jnp.sin(angles) * taps, axis=1))


def body(voltages, block_facet, block_tile, vis_offset, kernel_taps):
    facets = lax.axis_size("stn")
    chan_count = lax.axis_size("chan")
    high = lax.Precision.HIGHEST
    panels = lax.all_to_all(voltages, "stn", split_axis=1, concat_axis=0, tiled=True)
    stations = panels.shape[0]
    local_channels = panels.shape[1]
    samples = panels.shape[2] // 2
    swapped = jnp.concatenate([panels[:, :, samples:], -panels[:, :, :samples]], axis=2)
    stacked = jnp.concatenate([panels, swapped], axis=0)
    products = jnp.einsum("aks,jks->kaj", stacked, panels, preferred_element_type=jnp.float32)
    station_ids = jnp.arange(stations, dtype=jnp.int32)
    off_diagonal = (station_ids[:, None] != station_ids[None, :]).astype(jnp.float32)
    scale = 1.0 / math.sqrt(samples)
    real_vis = (products[:, :stations, :] * scale * off_diagonal).astype(jnp.bfloat16)
    imag_vis = (products[:, stations:, :] * scale * off_diagonal).astype(jnp.bfloat16)
    re = real_vis.reshape(-1, VB).astype(jnp.float32)
    im = imag_vis.reshape(-1, VB).astype(jnp.float32)
    block_count = re.shape[0]
    offsets = vis_offset.reshape(block_count, VB)
    du = offsets // OFFS
    dv = offsets % OFFS
    seg_ids = block_facet.reshape(block_count) * TT + block_tile.reshape(block_count)
    delta = grid_blocks(seg_ids, du, dv, re, im, facets)
    side = TS * TILE
    row_count = side // chan_count
    cosine, sine = dft_tables(side)
    along_x = jnp.stack(
        [jnp.stack([cosine, sine], axis=2), jnp.stack([-sine, cosine], axis=2)], axis=1
    ).reshape(2 * side, 2 * side)
    rows = jnp.einsum("kc,fcv->kfv", along_x, delta.reshape(facets, 2 * side, side), precision=high)
    rows = rows.reshape(chan_count, row_count * 2, facets, side)
    rows = jnp.transpose(rows, (2, 0, 1, 3)).reshape(facets * chan_count * row_count * 2, side)
    rows = lax.all_to_all(rows, ("stn", "chan"), split_axis=0, concat_axis=0, tiled=True)
    mine = jnp.sum(rows.reshape(facets * chan_count, row_count, 2, side), axis=0)
    along_y = jnp.stack(
        [jnp.stack([cosine, -sine], axis=1), jnp.stack([sine, cosine], axis=1)], axis=0
    )
    spectrum = jnp.einsum("rqv,qvsy->rsy", mine, along_y, precision=high)
    first_row = lax.axis_index("chan") * row_count
    u_re, u_im = taps_transform(kernel_taps[0], side)
    v_re, v_im = taps_transform(kernel_taps[1], side)
    u_re = lax.dynamic_slice_in_dim(u_re, first_row, row_count, 0)[:, None]
    u_im = lax.dynamic_slice_in_dim(u_im, first_row, row_count, 0)[:, None]
    k_re = u_re * v_re[None, :] - u_im * v_im[None, :]
    k_im = u_re * v_im[None, :] + u_im * v_re[None, :]
    s_re = spectrum[:, 0, :]
    s_im = spectrum[:, 1, :]
    channels_all = local_channels * facets * chan_count
    norm_factor = 1.0 / math.sqrt(channels_all * stations * stations * KT * KT / facets)
    image_re = (s_re * k_re - s_im * k_im) * norm_factor
    image_im = (s_re * k_im + s_im * k_re) * norm_factor
    return jnp.stack([image_re, image_im], axis=0)


def solution(mesh):
    placed = (
        P("stn", "chan", None),
        P("chan", "stn", None, None),
        P("chan", "stn", None),
        P("chan", "stn", None, None),
        P(),
    )
    return jax.shard_map(
        body, mesh=mesh, in_specs=placed, out_specs=P(None, ("stn", "chan"), None), check_vma=False
    )
```

```python
import functools
import math

import jax
import jax.numpy as jnp
from jax import lax
from jax.experimental import pallas as pl
from jax.experimental.pallas import tpu as pltpu
from jax.sharding import PartitionSpec as P

VB = 128
TILE = 32
KT = 8
TS = 4
TT = 16
OFFS = 25
CHUNK = 2048


def grid_kernel(seg_ref, du_ref, dv_ref, re_ref, im_ref, out_ref, acc_ref):
    step = pl.program_id(0)
    side = TS * TILE

    @pl.when(step == 0)
    def _():
        acc_ref[...] = jnp.zeros_like(acc_ref)

    cells = lax.broadcasted_iota(jnp.int32, (TILE, VB), 0)

    def one_block(b, carry):
        du = du_ref[pl.ds(b, 1), :]
        dv = dv_ref[pl.ds(b, 1), :]
        re = re_ref[pl.ds(b, 1), :]
        im = im_ref[pl.ds(b, 1), :]
        seg = seg_ref[step * CHUNK + b]
        facet = seg // TT
        tile = seg % TT
        first_u = pl.multiple_of((tile // TS) * TILE, TILE)
        along_u = (cells == du).astype(jnp.float32).astype(jnp.bfloat16)
        hit_v = cells == dv
        spread = jnp.concatenate(
            [jnp.where(hit_v, re, 0.0), jnp.where(hit_v, im, 0.0)], axis=0
        ).astype(jnp.bfloat16)
        tile_sum = lax.dot_general(
            along_u, spread, (((1,), (1,)), ((), ())), preferred_element_type=jnp.float32
        )
        acc_ref[facet, tile % TS, pl.ds(first_u, TILE), :] += tile_sum
        return carry

    lax.fori_loop(0, CHUNK, one_block, 0, unroll=64)

    @pl.when(step == pl.num_programs(0) - 1)
    def _():
        rows = lax.broadcasted_iota(jnp.int32, (2 * TILE, 2 * side), 0)
        cols = lax.broadcasted_iota(jnp.int32, (2 * TILE, 2 * side), 1)
        places = [
            (cols == (rows // TILE) * side + tv * TILE + rows % TILE).astype(jnp.float32).astype(jnp.bfloat16)
            for tv in range(TS)
        ]

        def one_facet(f, carry):
            total = jnp.zeros((side, 2 * side), jnp.float32)
            for tv in range(TS):
                part = acc_ref[f, tv]
                high = part.astype(jnp.bfloat16)
                low = (part - high.astype(jnp.float32)).astype(jnp.bfloat16)
                total = total + jnp.dot(high, places[tv], preferred_element_type=jnp.float32)
                total = total + jnp.dot(low, places[tv], preferred_element_type=jnp.float32)
            out_ref[f] = total
            return carry

        lax.fori_loop(0, out_ref.shape[0], one_facet, 0)


def grid_blocks(seg_ids, du, dv, re, im, facets):
    blocks = du.shape[0]
    side = TS * TILE
    row_spec = pl.BlockSpec((CHUNK, VB), lambda i, seg: (i, 0))
    return pl.pallas_call(
        grid_kernel,
        out_shape=jax.ShapeDtypeStruct((facets, side, 2 * side), jnp.float32),
        grid_spec=pltpu.PrefetchScalarGridSpec(
            num_scalar_prefetch=1,
            grid=(blocks // CHUNK,),
            in_specs=[row_spec] * 4,
            out_specs=pl.BlockSpec((facets, side, 2 * side), lambda i, seg: (0, 0, 0)),
            scratch_shapes=[pltpu.VMEM((facets, TS, side, 2 * TILE), jnp.float32)],
        ),
        cost_estimate=pl.CostEstimate(
            flops=blocks * TILE * VB * 2 * TILE * 2,
            bytes_accessed=blocks * VB * 16 + facets * side * 2 * side * 4,
            transcendentals=0,
        ),
    )(seg_ids, du, dv, re, im)


def dft_tables(side):
    index_ids = jnp.arange(side, dtype=jnp.int32)
    phases = index_ids[:, None] * index_ids[None, :] % side
    angles = phases.astype(jnp.float32) * (2.0 * math.pi / side)
    return (jnp.cos(angles), jnp.sin(angles))


def taps_transform(taps_row, side):
    index_ids = jnp.arange(side, dtype=jnp.int32)
    tap_ids = jnp.arange(KT, dtype=jnp.int32)
    phases = index_ids[:, None] * tap_ids[None, :] % side
    angles = phases.astype(jnp.float32) * (2.0 * math.pi / side)
    taps = taps_row.astype(jnp.float32)
    return (jnp.sum(jnp.cos(angles) * taps, axis=1), -jnp.sum(jnp.sin(angles) * taps, axis=1))


def body(voltages, block_facet, block_tile, vis_offset, kernel_taps):
    facets = lax.axis_size("stn")
    chan_count = lax.axis_size("chan")
    high = lax.Precision.HIGHEST
    panels = lax.all_to_all(voltages, "stn", split_axis=1, concat_axis=0, tiled=True)
    stations = panels.shape[0]
    local_channels = panels.shape[1]
    samples = panels.shape[2] // 2
    swapped = jnp.concatenate([panels[:, :, samples:], -panels[:, :, :samples]], axis=2)
    stacked = jnp.concatenate([panels, swapped], axis=0)
    products = jnp.einsum("aks,jks->kaj", stacked, panels, preferred_element_type=jnp.float32)
    station_ids = jnp.arange(stations, dtype=jnp.int32)
    off_diagonal = (station_ids[:, None] != station_ids[None, :]).astype(jnp.float32)
    scale = 1.0 / math.sqrt(samples)
    real_vis = (products[:, :stations, :] * scale * off_diagonal).astype(jnp.bfloat16)
    imag_vis = (products[:, stations:, :] * scale * off_diagonal).astype(jnp.bfloat16)
    re = real_vis.reshape(-1, VB).astype(jnp.float32)
    im = imag_vis.reshape(-1, VB).astype(jnp.float32)
    block_count = re.shape[0]
    offsets = vis_offset.reshape(block_count, VB)
    du = offsets // OFFS
    dv = offsets % OFFS
    seg_ids = block_facet.reshape(block_count) * TT + block_tile.reshape(block_count)
    delta = grid_blocks(seg_ids, du, dv, re, im, facets)
    side = TS * TILE
    row_count = side // chan_count
    cosine, sine = dft_tables(side)
    along_x = jnp.stack(
        [jnp.stack([cosine, sine], axis=2), jnp.stack([-sine, cosine], axis=2)], axis=1
    ).reshape(2 * side, 2 * side)
    rows = jnp.einsum("kc,fcv->kfv", along_x, delta.reshape(facets, 2 * side, side), precision=high)
    rows = rows.reshape(chan_count, row_count * 2, facets, side)
    rows = jnp.transpose(rows, (2, 0, 1, 3)).reshape(facets * chan_count * row_count * 2, side)
    rows = lax.all_to_all(rows, ("stn", "chan"), split_axis=0, concat_axis=0, tiled=True)
    mine = jnp.sum(rows.reshape(facets * chan_count, row_count, 2, side), axis=0)
    along_y = jnp.stack(
        [jnp.stack([cosine, -sine], axis=1), jnp.stack([sine, cosine], axis=1)], axis=0
    )
    spectrum = jnp.einsum("rqv,qvsy->rsy", mine, along_y, precision=high)
    first_row = lax.axis_index("chan") * row_count
    u_re, u_im = taps_transform(kernel_taps[0], side)
    v_re, v_im = taps_transform(kernel_taps[1], side)
    u_re = lax.dynamic_slice_in_dim(u_re, first_row, row_count, 0)[:, None]
    u_im = lax.dynamic_slice_in_dim(u_im, first_row, row_count, 0)[:, None]
    k_re = u_re * v_re[None, :] - u_im * v_im[None, :]
    k_im = u_re * v_im[None, :] + u_im * v_re[None, :]
    s_re = spectrum[:, 0, :]
    s_im = spectrum[:, 1, :]
    channels_all = local_channels * facets * chan_count
    norm_factor = 1.0 / math.sqrt(channels_all * stations * stations * KT * KT / facets)
    image_re = (s_re * k_re - s_im * k_im) * norm_factor
    image_im = (s_re * k_im + s_im * k_re) * norm_factor
    return jnp.stack([image_re, image_im], axis=0)


def solution(mesh):
    placed = (
        P("stn", "chan", None),
        P("chan", "stn", None, None),
        P("chan", "stn", None),
        P("chan", "stn", None, None),
        P(),
    )
    return jax.shard_map(
        body, mesh=mesh, in_specs=placed, out_specs=P(None, ("stn", "chan"), None), check_vma=False
    )
```

```python
import functools
import math

import jax
import jax.numpy as jnp
from jax import lax
from jax.experimental import pallas as pl
from jax.experimental.pallas import tpu as pltpu
from jax.sharding import PartitionSpec as P

VB = 128
TILE = 32
KT = 8
TS = 4
TT = 16
OFFS = 25
CHUNK = 2048


def grid_kernel(seg_ref, du_ref, dv_ref, re_ref, im_ref, out_ref, acc_ref):
    step = pl.program_id(0)
    side = TS * TILE

    @pl.when(step == 0)
    def _():
        acc_ref[...] = jnp.zeros_like(acc_ref)

    cells = lax.broadcasted_iota(jnp.int32, (TILE, VB), 0)

    def one_block(b, carry):
        du = du_ref[pl.ds(b, 1), :]
        dv = dv_ref[pl.ds(b, 1), :]
        re = re_ref[pl.ds(b, 1), :]
        im = im_ref[pl.ds(b, 1), :]
        seg = seg_ref[step * CHUNK + b]
        facet = seg // TT
        tile = seg % TT
        first_u = pl.multiple_of((tile // TS) * TILE, TILE)
        along_u = (cells == du).astype(jnp.float32).astype(jnp.bfloat16)
        hit_v = cells == dv
        spread = jnp.concatenate(
            [jnp.where(hit_v, re, 0.0), jnp.where(hit_v, im, 0.0)], axis=0
        ).astype(jnp.bfloat16)
        tile_sum = lax.dot_general(
            along_u, spread, (((1,), (1,)), ((), ())), preferred_element_type=jnp.float32
        )
        acc_ref[facet, tile % TS, pl.ds(first_u, TILE), :] += tile_sum
        return carry

    lax.fori_loop(0, CHUNK, one_block, 0, unroll=128)

    @pl.when(step == pl.num_programs(0) - 1)
    def _():
        rows = lax.broadcasted_iota(jnp.int32, (2 * TILE, 2 * side), 0)
        cols = lax.broadcasted_iota(jnp.int32, (2 * TILE, 2 * side), 1)
        places = [
            (cols == (rows // TILE) * side + tv * TILE + rows % TILE).astype(jnp.float32).astype(jnp.bfloat16)
            for tv in range(TS)
        ]

        def one_facet(f, carry):
            total = jnp.zeros((side, 2 * side), jnp.float32)
            for tv in range(TS):
                part = acc_ref[f, tv]
                high = part.astype(jnp.bfloat16)
                low = (part - high.astype(jnp.float32)).astype(jnp.bfloat16)
                total = total + jnp.dot(high, places[tv], preferred_element_type=jnp.float32)
                total = total + jnp.dot(low, places[tv], preferred_element_type=jnp.float32)
            out_ref[f] = total
            return carry

        lax.fori_loop(0, out_ref.shape[0], one_facet, 0)


def grid_blocks(seg_ids, du, dv, re, im, facets):
    blocks = du.shape[0]
    side = TS * TILE
    row_spec = pl.BlockSpec((CHUNK, VB), lambda i, seg: (i, 0))
    return pl.pallas_call(
        grid_kernel,
        out_shape=jax.ShapeDtypeStruct((facets, side, 2 * side), jnp.float32),
        grid_spec=pltpu.PrefetchScalarGridSpec(
            num_scalar_prefetch=1,
            grid=(blocks // CHUNK,),
            in_specs=[row_spec] * 4,
            out_specs=pl.BlockSpec((facets, side, 2 * side), lambda i, seg: (0, 0, 0)),
            scratch_shapes=[pltpu.VMEM((facets, TS, side, 2 * TILE), jnp.float32)],
        ),
        cost_estimate=pl.CostEstimate(
            flops=blocks * TILE * VB * 2 * TILE * 2,
            bytes_accessed=blocks * VB * 16 + facets * side * 2 * side * 4,
            transcendentals=0,
        ),
    )(seg_ids, du, dv, re, im)


def dft_tables(side):
    index_ids = jnp.arange(side, dtype=jnp.int32)
    phases = index_ids[:, None] * index_ids[None, :] % side
    angles = phases.astype(jnp.float32) * (2.0 * math.pi / side)
    return (jnp.cos(angles), jnp.sin(angles))


def taps_transform(taps_row, side):
    index_ids = jnp.arange(side, dtype=jnp.int32)
    tap_ids = jnp.arange(KT, dtype=jnp.int32)
    phases = index_ids[:, None] * tap_ids[None, :] % side
    angles = phases.astype(jnp.float32) * (2.0 * math.pi / side)
    taps = taps_row.astype(jnp.float32)
    return (jnp.sum(jnp.cos(angles) * taps, axis=1), -jnp.sum(jnp.sin(angles) * taps, axis=1))


def body(voltages, block_facet, block_tile, vis_offset, kernel_taps):
    facets = lax.axis_size("stn")
    chan_count = lax.axis_size("chan")
    high = lax.Precision.HIGHEST
    panels = lax.all_to_all(voltages, "stn", split_axis=1, concat_axis=0, tiled=True)
    stations = panels.shape[0]
    local_channels = panels.shape[1]
    samples = panels.shape[2] // 2
    swapped = jnp.concatenate([panels[:, :, samples:], -panels[:, :, :samples]], axis=2)
    stacked = jnp.concatenate([panels, swapped], axis=0)
    products = jnp.einsum("aks,jks->kaj", stacked, panels, preferred_element_type=jnp.float32)
    station_ids = jnp.arange(stations, dtype=jnp.int32)
    off_diagonal = (station_ids[:, None] != station_ids[None, :]).astype(jnp.float32)
    scale = 1.0 / math.sqrt(samples)
    real_vis = (products[:, :stations, :] * scale * off_diagonal).astype(jnp.bfloat16)
    imag_vis = (products[:, stations:, :] * scale * off_diagonal).astype(jnp.bfloat16)
    re = real_vis.reshape(-1, VB).astype(jnp.float32)
    im = imag_vis.reshape(-1, VB).astype(jnp.float32)
    block_count = re.shape[0]
    offsets = vis_offset.reshape(block_count, VB)
    du = offsets // OFFS
    dv = offsets % OFFS
    seg_ids = block_facet.reshape(block_count) * TT + block_tile.reshape(block_count)
    delta = grid_blocks(seg_ids, du, dv, re, im, facets)
    side = TS * TILE
    row_count = side // chan_count
    cosine, sine = dft_tables(side)
    along_x = jnp.stack(
        [jnp.stack([cosine, sine], axis=2), jnp.stack([-sine, cosine], axis=2)], axis=1
    ).reshape(2 * side, 2 * side)
    rows = jnp.einsum("kc,fcv->kfv", along_x, delta.reshape(facets, 2 * side, side), precision=high)
    rows = rows.reshape(chan_count, row_count * 2, facets, side)
    rows = jnp.transpose(rows, (2, 0, 1, 3)).reshape(facets * chan_count * row_count * 2, side)
    rows = lax.all_to_all(rows, ("stn", "chan"), split_axis=0, concat_axis=0, tiled=True)
    mine = jnp.sum(rows.reshape(facets * chan_count, row_count, 2, side), axis=0)
    along_y = jnp.stack(
        [jnp.stack([cosine, -sine], axis=1), jnp.stack([sine, cosine], axis=1)], axis=0
    )
    spectrum = jnp.einsum("rqv,qvsy->rsy", mine, along_y, precision=high)
    first_row = lax.axis_index("chan") * row_count
    u_re, u_im = taps_transform(kernel_taps[0], side)
    v_re, v_im = taps_transform(kernel_taps[1], side)
    u_re = lax.dynamic_slice_in_dim(u_re, first_row, row_count, 0)[:, None]
    u_im = lax.dynamic_slice_in_dim(u_im, first_row, row_count, 0)[:, None]
    k_re = u_re * v_re[None, :] - u_im * v_im[None, :]
    k_im = u_re * v_im[None, :] + u_im * v_re[None, :]
    s_re = spectrum[:, 0, :]
    s_im = spectrum[:, 1, :]
    channels_all = local_channels * facets * chan_count
    norm_factor = 1.0 / math.sqrt(channels_all * stations * stations * KT * KT / facets)
    image_re = (s_re * k_re - s_im * k_im) * norm_factor
    image_im = (s_re * k_im + s_im * k_re) * norm_factor
    return jnp.stack([image_re, image_im], axis=0)


def solution(mesh):
    placed = (
        P("stn", "chan", None),
        P("chan", "stn", None, None),
        P("chan", "stn", None),
        P("chan", "stn", None, None),
        P(),
    )
    return jax.shard_map(
        body, mesh=mesh, in_specs=placed, out_specs=P(None, ("stn", "chan"), None), check_vma=False
    )
```

```python
import functools
import math

import jax
import jax.numpy as jnp
from jax import lax
from jax.experimental import pallas as pl
from jax.experimental.pallas import tpu as pltpu
from jax.sharding import PartitionSpec as P

VB = 128
TILE = 32
KT = 8
TS = 4
TT = 16
OFFS = 25
CHUNK = 2048


def grid_kernel(seg_ref, du_ref, re_ref, im_ref, out_ref, acc_ref):
    step = pl.program_id(0)
    side = TS * TILE

    @pl.when(step == 0)
    def _():
        acc_ref[...] = jnp.zeros_like(acc_ref)

    cells = lax.broadcasted_iota(jnp.int32, (TILE, VB), 0)

    def one_block(b, carry):
        code = du_ref[pl.ds(b, 1), :]
        du = code // TILE
        dv = code % TILE
        re = re_ref[pl.ds(b, 1), :]
        im = im_ref[pl.ds(b, 1), :]
        seg = seg_ref[step * CHUNK + b]
        facet = seg // TT
        tile = seg % TT
        first_u = pl.multiple_of((tile // TS) * TILE, TILE)
        along_u = (cells == du).astype(jnp.float32).astype(jnp.bfloat16)
        hit_v = cells == dv
        spread = jnp.concatenate(
            [jnp.where(hit_v, re, 0.0), jnp.where(hit_v, im, 0.0)], axis=0
        ).astype(jnp.bfloat16)
        tile_sum = lax.dot_general(
            along_u, spread, (((1,), (1,)), ((), ())), preferred_element_type=jnp.float32
        )
        acc_ref[facet, tile % TS, pl.ds(first_u, TILE), :] += tile_sum
        return carry

    lax.fori_loop(0, CHUNK, one_block, 0, unroll=128)

    @pl.when(step == pl.num_programs(0) - 1)
    def _():
        rows = lax.broadcasted_iota(jnp.int32, (2 * TILE, 2 * side), 0)
        cols = lax.broadcasted_iota(jnp.int32, (2 * TILE, 2 * side), 1)
        places = [
            (cols == (rows // TILE) * side + tv * TILE + rows % TILE).astype(jnp.float32).astype(jnp.bfloat16)
            for tv in range(TS)
        ]

        def one_facet(f, carry):
            total = jnp.zeros((side, 2 * side), jnp.float32)
            for tv in range(TS):
                part = acc_ref[f, tv]
                high = part.astype(jnp.bfloat16)
                low = (part - high.astype(jnp.float32)).astype(jnp.bfloat16)
                total = total + jnp.dot(high, places[tv], preferred_element_type=jnp.float32)
                total = total + jnp.dot(low, places[tv], preferred_element_type=jnp.float32)
            out_ref[f] = total
            return carry

        lax.fori_loop(0, out_ref.shape[0], one_facet, 0)


def grid_blocks(seg_ids, du, re, im, facets):
    blocks = du.shape[0]
    side = TS * TILE
    row_spec = pl.BlockSpec((CHUNK, VB), lambda i, seg: (i, 0))
    return pl.pallas_call(
        grid_kernel,
        out_shape=jax.ShapeDtypeStruct((facets, side, 2 * side), jnp.float32),
        grid_spec=pltpu.PrefetchScalarGridSpec(
            num_scalar_prefetch=1,
            grid=(blocks // CHUNK,),
            in_specs=[row_spec] * 3,
            out_specs=pl.BlockSpec((facets, side, 2 * side), lambda i, seg: (0, 0, 0)),
            scratch_shapes=[pltpu.VMEM((facets, TS, side, 2 * TILE), jnp.float32)],
        ),
        cost_estimate=pl.CostEstimate(
            flops=blocks * TILE * VB * 2 * TILE * 2,
            bytes_accessed=blocks * VB * 16 + facets * side * 2 * side * 4,
            transcendentals=0,
        ),
    )(seg_ids, du, re, im)


def dft_tables(side):
    index_ids = jnp.arange(side, dtype=jnp.int32)
    phases = index_ids[:, None] * index_ids[None, :] % side
    angles = phases.astype(jnp.float32) * (2.0 * math.pi / side)
    return (jnp.cos(angles), jnp.sin(angles))


def taps_transform(taps_row, side):
    index_ids = jnp.arange(side, dtype=jnp.int32)
    tap_ids = jnp.arange(KT, dtype=jnp.int32)
    phases = index_ids[:, None] * tap_ids[None, :] % side
    angles = phases.astype(jnp.float32) * (2.0 * math.pi / side)
    taps = taps_row.astype(jnp.float32)
    return (jnp.sum(jnp.cos(angles) * taps, axis=1), -jnp.sum(jnp.sin(angles) * taps, axis=1))


def body(voltages, block_facet, block_tile, vis_offset, kernel_taps):
    facets = lax.axis_size("stn")
    chan_count = lax.axis_size("chan")
    high = lax.Precision.HIGHEST
    panels = lax.all_to_all(voltages, "stn", split_axis=1, concat_axis=0, tiled=True)
    stations = panels.shape[0]
    local_channels = panels.shape[1]
    samples = panels.shape[2] // 2
    swapped = jnp.concatenate([panels[:, :, samples:], -panels[:, :, :samples]], axis=2)
    stacked = jnp.concatenate([panels, swapped], axis=0)
    products = jnp.einsum("aks,jks->kaj", stacked, panels, preferred_element_type=jnp.float32)
    station_ids = jnp.arange(stations, dtype=jnp.int32)
    off_diagonal = (station_ids[:, None] != station_ids[None, :]).astype(jnp.float32)
    scale = 1.0 / math.sqrt(samples)
    real_vis = (products[:, :stations, :] * scale * off_diagonal).astype(jnp.bfloat16)
    imag_vis = (products[:, stations:, :] * scale * off_diagonal).astype(jnp.bfloat16)
    re = real_vis.reshape(-1, VB).astype(jnp.float32)
    im = imag_vis.reshape(-1, VB).astype(jnp.float32)
    block_count = re.shape[0]
    offsets = vis_offset.reshape(block_count, VB)
    du = offsets // OFFS
    dv = offsets % OFFS
    seg_ids = block_facet.reshape(block_count) * TT + block_tile.reshape(block_count)
    delta = grid_blocks(seg_ids, du * TILE + dv, re, im, facets)
    side = TS * TILE
    row_count = side // chan_count
    cosine, sine = dft_tables(side)
    along_x = jnp.stack(
        [jnp.stack([cosine, sine], axis=2), jnp.stack([-sine, cosine], axis=2)], axis=1
    ).reshape(2 * side, 2 * side)
    rows = jnp.einsum("kc,fcv->kfv", along_x, delta.reshape(facets, 2 * side, side), precision=high)
    rows = rows.reshape(chan_count, row_count * 2, facets, side)
    rows = jnp.transpose(rows, (2, 0, 1, 3)).reshape(facets * chan_count * row_count * 2, side)
    rows = lax.all_to_all(rows, ("stn", "chan"), split_axis=0, concat_axis=0, tiled=True)
    mine = jnp.sum(rows.reshape(facets * chan_count, row_count, 2, side), axis=0)
    along_y = jnp.stack(
        [jnp.stack([cosine, -sine], axis=1), jnp.stack([sine, cosine], axis=1)], axis=0
    )
    spectrum = jnp.einsum("rqv,qvsy->rsy", mine, along_y, precision=high)
    first_row = lax.axis_index("chan") * row_count
    u_re, u_im = taps_transform(kernel_taps[0], side)
    v_re, v_im = taps_transform(kernel_taps[1], side)
    u_re = lax.dynamic_slice_in_dim(u_re, first_row, row_count, 0)[:, None]
    u_im = lax.dynamic_slice_in_dim(u_im, first_row, row_count, 0)[:, None]
    k_re = u_re * v_re[None, :] - u_im * v_im[None, :]
    k_im = u_re * v_im[None, :] + u_im * v_re[None, :]
    s_re = spectrum[:, 0, :]
    s_im = spectrum[:, 1, :]
    channels_all = local_channels * facets * chan_count
    norm_factor = 1.0 / math.sqrt(channels_all * stations * stations * KT * KT / facets)
    image_re = (s_re * k_re - s_im * k_im) * norm_factor
    image_im = (s_re * k_im + s_im * k_re) * norm_factor
    return jnp.stack([image_re, image_im], axis=0)


def solution(mesh):
    placed = (
        P("stn", "chan", None),
        P("chan", "stn", None, None),
        P("chan", "stn", None),
        P("chan", "stn", None, None),
        P(),
    )
    return jax.shard_map(
        body, mesh=mesh, in_specs=placed, out_specs=P(None, ("stn", "chan"), None), check_vma=False
    )
```
